512 devices in a mesh: dp: 16 (over z, core), tp: 32 (over y, x).
Axes of the slice: x: 4, y: 8, z: 8, core: 2. Of those that a mesh axis runs over, the one named last changes fastest.
Arguments:
- q_new: bfloat16 [512, 1536], P(('dp', 'tp'))
- new_key_value: bfloat16 [512, 512], P(('dp', 'tp')), may hold values from -6 to 6
- resid_dec: bfloat16 [512, 1536], P(('dp', 'tp')), may hold values from -6 to 6
- placing: int32 [512], replicated, may hold values from 0 to 511, as said below
- lengths: int32 [512], P('dp'), may hold values from 5 to 2048, as said below
- write_pos: int32 [512], P('dp'), may hold values from 4 to 2047, as said below
- k_cache: bfloat16 [512, 2, 2048, 128], P('dp', None, 'tp')
- value_cache: bfloat16 [512, 2, 2048, 128], P('dp', None, 'tp'), may hold values from -6 to 6
- w_out: bfloat16 [1536, 1536], P(None, 'tp'), may hold values from -0.15625 to 0.15625
- x_pre: bfloat16 [32256, 1536], P(('dp', 'tp')), may hold values from -6 to 6
- routes: int32 [32768, 4], P(('dp', 'tp')), may hold values from 0 to 31, all different within a row; in each aligned block of 64 rows (0 to 63, 64 to 127, ...) at most 16 rows name the same one
- route_scale: float32 [32768, 4], P(('dp', 'tp')), may hold values from 0.2 to 2
- moe_gain: float32 [1536], replicated, may hold values from 0.5 to 1.5
- w_gate: bfloat16 [32, 768, 1536], P('tp', 'dp'), may hold values from -0.15625 to 0.15625
- w_up: bfloat16 [32, 768, 1536], P('tp', 'dp'), may hold values from -0.15625 to 0.15625
- w_down: bfloat16 [32, 768, 1536], P('tp', 'dp'), may hold values from -0.21875 to 0.21875
Outputs:
- out_pre: bfloat16 [32256, 1536], P(('dp', 'tp'))
- out_dec: bfloat16 [512, 1536], P(('dp', 'tp'))
The draws below stay inside these ranges and needn't reach their ends.
Inputs may be any that keep to these rules, and one draw needn't show every extreme that they name: Each of 0 to 511 appears once; cache row j belongs to request placing[j]. `lengths`: a cache row is either full (2048 live slots) or filled from slot 0 up; some row is full. `write_pos`: below the row's length; a row that is not full writes at its length - 1, a full row anywhere past the sink slots. `routes`: the 64 rows of one device name any one expert at most 16 times.
All inputs are finite; a program needn't handle non-finite values.
Results may differ from the reference program's by a relative error of at most 0.007.
Values may be sent and summed in bfloat16 or wider, within the bound.
No kernel may reach another device: no remote copies, remote signals or barrier semaphores. Data moves between devices by JAX's collectives and lax.ppermute only.
A program may use at most 64 MiB of HBM per device.

```python
import math
import jax
import jax.numpy as jnp
import numpy as np
from jax import lax

D = 1536
QUERY_HEADS = 12
KEY_VALUE_HEADS = 2
HEAD_WIDTH = 128
FF = 768
TOPK = 4
EXPERTS = 32
SINK = 4
CACHE_SLOTS = 2048
PRE_DEV = 63
ROWS_DEV = 64
DECODE_REQUESTS = 512
PRE_TOK = 32256
ROWS_TOK = 32768
CAP = 16
N_DP = 16
N_TP = 32


def cache_fill(key):
    inner_key = jax.random.fold_in(key, 5)
    leading_key, following_key, third_key = jax.random.split(inner_key, 3)
    is_full = jax.random.randint(leading_key, (DECODE_REQUESTS,), 0, 2) == 1
    is_full = is_full.at[0].set(True)
    short_len = jax.random.randint(following_key, (DECODE_REQUESTS,), SINK + 1, CACHE_SLOTS)
    length = jnp.where(is_full, CACHE_SLOTS, short_len)
    cycle_slot = jax.random.randint(third_key, (DECODE_REQUESTS,), SINK, CACHE_SLOTS)
    write_at = jnp.where(is_full, cycle_slot, length - 1)
    return (length.astype(jnp.int32), write_at.astype(jnp.int32))


def draw_placing(key, part):
    return jax.random.permutation(jax.random.fold_in(key, 3), DECODE_REQUESTS).astype(jnp.int32)


def draw_lengths(key, part):
    return cache_fill(key)[0]


def draw_write_pos(key, part):
    return cache_fill(key)[1]


def draw_k_cache(key, part):
    sampled_draw = jax.random.normal(jax.random.fold_in(key, 21), (DECODE_REQUESTS, KEY_VALUE_HEADS, CACHE_SLOTS, HEAD_WIDTH), jnp.float32)
    return sampled_draw.astype(jnp.bfloat16)


def draw_q_new(key, part):
    sampled_draw = jax.random.normal(jax.random.fold_in(key, 23), (DECODE_REQUESTS, QUERY_HEADS * HEAD_WIDTH), jnp.float32)
    return sampled_draw.astype(jnp.bfloat16)


def shard_levels(own_key, dims, pieces, low, largest):
    factor_of = 1.0
    for axis_at, parts in pieces:
        draws = jax.random.uniform(jax.random.fold_in(jax.random.fold_in(own_key, 6), axis_at), (parts,), jnp.float32, low / len(pieces), largest / len(pieces))
        factor_of = factor_of * jnp.repeat(jnp.exp(draws), dims[axis_at] // parts).reshape((-1,) + (1,) * (len(dims) - 1 - axis_at))
    return factor_of


def assign_block(stream_key, own, number, rows, number_of, top, bound, skew):
    ranking = jax.random.permutation(stream_key, number_of)
    crowded, usual = load_shares(number_of, rows * top, bound, skew, True), load_shares(number_of, rows * top, bound, skew, False)
    places = jnp.arange(number_of)

    def named(tallies, rotation):
        used = int((tallies > 0).sum())
        fixed = max(1, used // 4)
        moved = fixed + (places - fixed + rotation * (used - fixed)) % max(1, number_of - fixed)
        return jnp.zeros((number_of,), jnp.int32).at[ranking[jnp.where(places < fixed, places, moved)]].set(jnp.asarray(tallies, jnp.int32))

    tallies = jnp.where(number % 4 == 0, named(crowded, number // 4), named(usual, number - number // 4 - 1))
    mixed = jax.random.permutation(jax.random.fold_in(own, 3), number_of)
    donor, sink = mixed[0:number_of // 2 * 2:2], mixed[1:number_of // 2 * 2:2]
    slack = jnp.minimum(tallies[donor] - 1, bound - tallies[sink]) // 2
    slack = jnp.where((donor == ranking[0]) | (sink == ranking[0]) | (tallies[sink] == 0), 0, jnp.maximum(slack, 0))
    moved = jax.random.randint(jax.random.fold_in(own, 4), (number_of // 2,), 0, 1 << 20) % (slack + 1)
    tallies = tallies.at[donor].add(-moved).at[sink].add(moved)
    members = jnp.searchsorted(jnp.cumsum(tallies), jnp.arange(rows * top), side="right").astype(jnp.int32)
    grid = members.reshape(top, rows).T
    grid = grid[jax.random.permutation(jax.random.fold_in(own, 1), rows)]
    rotation = jax.random.randint(jax.random.fold_in(own, 2), (rows, 1), 0, top)
    return jnp.take_along_axis(grid, (jnp.arange(top)[None, :] + rotation) % top, axis=1)


def load_shares(count, total, bound, slope, full):
    weights = [(1 << 20) // math.isqrt(grade ** slope) + 1 for grade in range(1, count + 1)]
    largest = bound if full else min(bound, max(-(-total // count), total * weights[0] // sum(weights)))
    least = 1 if total - largest >= count - 1 else 0
    given, surplus = [largest] + [least] * (count - 1), total - largest - least * (count - 1)
    while surplus > 0:
        free = [i for i in range(1, count) if given[i] < largest] or [i for i in range(1, count) if given[i] < bound]
        pool, left = sum([weights[i] for i in free]), surplus
        for i in free:
            addition = min(bound - given[i], max(1, left * weights[i] // pool), surplus)
            given[i] = given[i] + addition
            surplus = surplus - addition
    return np.array(given)


def normal_values(stream_key, dims, width, most, cuts=(), held_as=jnp.bfloat16):
    level = shard_levels(stream_key, dims, cuts, -0.22, 0.18) if cuts else 1.0
    values = jax.random.normal(stream_key, dims, jnp.float32) * width * level
    return jnp.minimum(jnp.maximum(values, -most), most).astype(held_as)


def setup_inputs(seed: int = 0) -> dict:
    arg_keys = jax.random.split(jax.random.key(seed), 17)
    q_new = draw_q_new(jax.random.fold_in(arg_keys[16], 71), 0)
    new_key_value = normal_values(arg_keys[1], (DECODE_REQUESTS, 2 * KEY_VALUE_HEADS * HEAD_WIDTH), 1.0, 6.0, ((0, 512),))
    resid_dec = normal_values(arg_keys[2], (DECODE_REQUESTS, D), 1.0, 6.0, ((0, 512),))
    placing = draw_placing(jax.random.fold_in(arg_keys[16], 71), 0)
    lengths = draw_lengths(jax.random.fold_in(arg_keys[16], 71), 0)
    write_pos = draw_write_pos(jax.random.fold_in(arg_keys[16], 71), 0)
    k_cache = draw_k_cache(jax.random.fold_in(arg_keys[16], 71), 0)
    value_cache = normal_values(arg_keys[7], (DECODE_REQUESTS, KEY_VALUE_HEADS, CACHE_SLOTS, HEAD_WIDTH), 1.0, 6.0, ((0, 16), (2, 32)))
    w_out = normal_values(arg_keys[8], (QUERY_HEADS * HEAD_WIDTH, D), (QUERY_HEADS * HEAD_WIDTH) ** -0.5, 0.15625, ((1, 32),))
    x_pre = normal_values(arg_keys[9], (PRE_TOK, D), 1.0, 6.0, ((0, 512),))
    routes_keys = jax.random.split(jax.random.fold_in(arg_keys[10], 1), ROWS_TOK // ROWS_DEV)
    routes_turns = jax.random.permutation(jax.random.fold_in(arg_keys[10], 3), ROWS_TOK // ROWS_DEV)
    routes = jax.vmap(lambda own, number: assign_block(jax.random.fold_in(arg_keys[10], 2), own, number, ROWS_DEV, EXPERTS, TOPK, CAP, 1))(routes_keys, routes_turns).reshape((ROWS_TOK, TOPK))
    route_scale = jnp.clip(jnp.exp(math.log(2.0) - 2.3025851 * jax.random.uniform(arg_keys[11], (ROWS_TOK, TOPK), jnp.float32) ** shard_levels(arg_keys[11], (ROWS_TOK, TOPK), ((0, 512),), -0.2, 0.2)), 0.2, 2.0)
    moe_gain = jnp.clip(1.0 + 0.1 * jax.random.normal(arg_keys[12], (D,), jnp.float32), 0.5, 1.5)
    w_gate = normal_values(arg_keys[13], (EXPERTS, FF, D), D ** -0.5, 0.15625, ((0, 32), (1, 16)))
    w_up = normal_values(arg_keys[14], (EXPERTS, FF, D), D ** -0.5, 0.15625, ((0, 32), (1, 16)))
    w_down = normal_values(arg_keys[15], (EXPERTS, FF, D), FF ** -0.5, 0.21875, ((0, 32), (1, 16)))
    return {"q_new": q_new, "new_key_value": new_key_value, "resid_dec": resid_dec, "placing": placing, "lengths": lengths, "write_pos": write_pos, "k_cache": k_cache, "value_cache": value_cache, "w_out": w_out, "x_pre": x_pre, "routes": routes, "route_scale": route_scale, "moe_gain": moe_gain, "w_gate": w_gate, "w_up": w_up, "w_down": w_down}


HIGHEST = lax.Precision.HIGHEST

def attend_row(inputs):
    current_query_row, incoming_row, key_rows, value_rows, length, write_at = inputs
    slot_ids = jnp.arange(CACHE_SLOTS, dtype=jnp.int32)
    incoming_key = incoming_row[:KEY_VALUE_HEADS * HEAD_WIDTH].reshape(KEY_VALUE_HEADS, 1, HEAD_WIDTH)
    incoming_value = incoming_row[KEY_VALUE_HEADS * HEAD_WIDTH:].reshape(KEY_VALUE_HEADS, 1, HEAD_WIDTH)
    written = (slot_ids == write_at)[None, :, None]
    key_all = jnp.where(written, incoming_key, key_rows).astype(jnp.float32)
    value_all = jnp.where(written, incoming_value, value_rows).astype(jnp.float32)
    query_head_list = current_query_row.reshape(KEY_VALUE_HEADS, QUERY_HEADS // KEY_VALUE_HEADS, HEAD_WIDTH).astype(jnp.float32)
    scores = jnp.einsum('gqd,gsd->gqs', query_head_list, key_all, precision=HIGHEST) * HEAD_WIDTH ** (-0.5)
    is_valid = (slot_ids < length)[None, None, :]
    masked = jnp.where(is_valid, scores, -1e+30)
    peak = lax.optimization_barrier(jnp.max(masked, axis=-1, keepdims=True))
    weights = jnp.where(is_valid, jnp.exp(masked - peak), 0.0)
    weight_total = lax.optimization_barrier(jnp.sum(weights, axis=-1))
    mixed_sum = jnp.einsum('gqs,gsd->gqd', weights, value_all, precision=HIGHEST)
    return (mixed_sum / weight_total[..., None]).reshape(QUERY_HEADS * HEAD_WIDTH).astype(jnp.bfloat16)

def reference(q_new, new_key_value, resid_dec, placing, lengths, write_pos, k_cache, value_cache, w_out, x_pre, routes, route_scale, moe_gain, w_gate, w_up, w_down):
    cached_query = jnp.take(q_new, placing, axis=0)
    cached_new = jnp.take(new_key_value, placing, axis=0)
    attention = lax.map(attend_row, (cached_query, cached_new, k_cache, value_cache, lengths, write_pos))
    projected = jnp.dot(attention, w_out, preferred_element_type=jnp.float32).astype(jnp.bfloat16)
    positions = jnp.arange(DECODE_REQUESTS, dtype=jnp.int32)
    home_index = jnp.zeros((DECODE_REQUESTS,), jnp.int32).at[placing].set(positions)
    proj_home = jnp.take(projected, home_index, axis=0)
    hidden_dec = (resid_dec.astype(jnp.float32) + proj_home.astype(jnp.float32)).astype(jnp.bfloat16)
    devices = N_DP * N_TP
    moe_rows = jnp.concatenate([x_pre.reshape(devices, PRE_DEV, D), hidden_dec.reshape(devices, 1, D)], axis=1).reshape(ROWS_TOK, D)
    rows_f32 = moe_rows.astype(jnp.float32)
    mean_square = lax.optimization_barrier(jnp.mean(rows_f32 * rows_f32, axis=-1, keepdims=True))
    normed = (rows_f32 * lax.rsqrt(mean_square + 1e-06) * moe_gain).astype(jnp.bfloat16)
    route_weight = route_scale / lax.optimization_barrier(jnp.sum(route_scale, axis=-1, keepdims=True))
    expert_ids = routes.reshape(devices, ROWS_DEV * TOPK)
    onehot = (expert_ids[:, :, None] == jnp.arange(EXPERTS, dtype=jnp.int32)[None, None, :]).astype(jnp.int32)
    position = lax.optimization_barrier(jnp.sum(onehot * (jnp.cumsum(onehot, axis=1) - onehot), axis=-1))
    slot_index = (expert_ids * CAP + position).astype(jnp.int32)
    device_ids = jnp.broadcast_to(jnp.arange(devices, dtype=jnp.int32)[:, None], slot_index.shape)
    source_row = (device_ids * ROWS_DEV + jnp.arange(ROWS_DEV * TOPK, dtype=jnp.int32)[None, :] // TOPK).astype(jnp.int32)
    row_table = jnp.zeros((devices, EXPERTS * CAP), jnp.int32).at[device_ids, slot_index].set(source_row)
    weight_table = jnp.zeros((devices, EXPERTS * CAP), jnp.float32).at[device_ids, slot_index].set(route_weight.reshape(devices, ROWS_DEV * TOPK))
    row_table = row_table.reshape(devices, EXPERTS, CAP).transpose(1, 0, 2).reshape(EXPERTS, devices * CAP)
    weight_table = weight_table.reshape(devices, EXPERTS, CAP).transpose(1, 0, 2).reshape(EXPERTS, devices * CAP)

    def one_expert(running, inputs):
        gate_rows, up_rows, down_rows, row_ids, weight_ids = inputs
        picked = jnp.take(normed, row_ids, axis=0)
        gate = jnp.dot(picked, gate_rows.T, preferred_element_type=jnp.float32)
        upper = jnp.dot(picked, up_rows.T, preferred_element_type=jnp.float32)
        active = (jnp.maximum(gate, 0.0) * upper).astype(jnp.bfloat16)
        expert_out = jnp.dot(active, down_rows, preferred_element_type=jnp.float32).astype(jnp.bfloat16)
        running = running.at[row_ids].add(weight_ids[:, None] * expert_out.astype(jnp.float32))
        return (running, None)
    mixture, _ = lax.scan(one_expert, jnp.zeros((ROWS_TOK, D), jnp.float32), (w_gate, w_up, w_down, row_table, weight_table))
    moe_out = (rows_f32 + mixture).astype(jnp.bfloat16).reshape(devices, ROWS_DEV, D)
    out_pre = moe_out[:, :PRE_DEV].reshape(PRE_TOK, D)
    out_dec = moe_out[:, PRE_DEV]
    return (out_pre, out_dec)
```

```python
import jax
import jax.numpy as jnp
from jax import lax
from jax.sharding import PartitionSpec as P

HIGHEST = lax.Precision.HIGHEST
F32 = jnp.float32
BF16 = jnp.bfloat16


def contract_rows(left_rows, unit_rows):
    return lax.dot_general(
        left_rows, unit_rows, (((1,), (1,)), ((), ())), preferred_element_type=F32
    )


def swap(blocks, axis_name):
    return lax.all_to_all(blocks, axis_name, split_axis=0, concat_axis=0, tiled=True)


def spread(block, axis_name):
    members = lax.axis_size(axis_name)
    return swap(jnp.broadcast_to(block[None], (members,) + block.shape), axis_name)


def choose_rows(table, rows):
    return jnp.dot(table.astype(BF16), rows, preferred_element_type=F32).astype(BF16)


def pieces_of(x):
    high = lax.reduce_precision(x, 8, 7)
    middle = lax.reduce_precision(x - high, 8, 7)
    low = lax.reduce_precision(x - high - middle, 8, 7)
    return high.astype(BF16), middle.astype(BF16), low.astype(BF16)


def rms(rows_f32, gain):
    mean_square = jnp.mean(rows_f32 * rows_f32, axis=-1, keepdims=True)
    return (rows_f32 * lax.rsqrt(mean_square + 1e-06) * gain).astype(BF16)


def expert_units(rows, units):
    gate = contract_rows(rows, units[0])
    upper = contract_rows(rows, units[1])
    active = (jnp.maximum(gate, 0.0) * upper).astype(BF16)
    return jnp.dot(active, units[2], preferred_element_type=F32).astype(BF16)


def on_device(
    q_new,
    new_key_value,
    resid_dec,
    placing,
    lengths,
    write_pos,
    k_cache,
    value_cache,
    w_out,
    x_pre,
    routes,
    route_scale,
    moe_gain,
    w_gate,
    w_up,
    w_down,
):
    dp_size = lax.axis_size("dp")
    tp_size = lax.axis_size("tp")
    dp_group = lax.axis_index("dp")
    tp_lane = lax.axis_index("tp")
    group_reqs, kv_heads, slot_dev, head_size = k_cache.shape
    width = q_new.shape[1]
    heads = width // head_size
    per_group = heads // kv_heads
    total_reqs = placing.shape[0]
    experts = tp_size * w_gate.shape[0]
    assert group_reqs == tp_size and experts == tp_size

    units = lax.all_gather(
        jnp.concatenate([w_gate, w_up, w_down], axis=0), "dp", axis=1, tiled=True
    )

    columns = heads + 2 * kv_heads
    share = tp_size // columns
    chosen_rows = group_reqs // share
    fresh = jnp.concatenate([q_new, new_key_value], axis=1).reshape(1, columns, 1, head_size)
    by_head = swap(
        jnp.broadcast_to(fresh, (share, columns, 1, head_size)).reshape(tp_size, 1, head_size), "tp"
    )
    all_rows = spread(by_head.reshape(tp_size, head_size), "dp").reshape(total_reqs, head_size)
    first_row = dp_group * group_reqs + (tp_lane // columns) * chosen_rows
    wanted = lax.dynamic_slice_in_dim(placing, first_row, chosen_rows)
    request_ids = jnp.arange(total_reqs, dtype=jnp.int32)
    mine = choose_rows(wanted[:, None] == request_ids[None, :], all_rows)
    heads_here = spread(mine, "tp").reshape(share, columns, chosen_rows, head_size)
    cached = jnp.transpose(heads_here, (0, 2, 1, 3)).reshape(group_reqs, columns, head_size)
    query_head_list = cached[:, :heads].reshape(group_reqs, kv_heads, per_group, head_size)
    incoming_key = cached[:, heads : heads + kv_heads][:, :, None, :]
    incoming_value = cached[:, heads + kv_heads :][:, :, None, :]

    slot_ids = tp_lane * slot_dev + jnp.arange(slot_dev, dtype=jnp.int32)
    written = (slot_ids[None, :] == write_pos[:, None])[:, None, :, None]
    key_rows = jnp.where(written, incoming_key, k_cache)
    value_rows = jnp.where(written, incoming_value, value_cache).astype(F32)
    scores = jnp.einsum(
        "rgqd,rgsd->rgqs", query_head_list, key_rows, preferred_element_type=F32
    ) * head_size ** (-0.5)
    is_valid = (slot_ids[None, :] < lengths[:, None])[:, None, None, :]
    masked = jnp.where(is_valid, scores, -1e30)
    local_peak = jnp.max(masked, axis=-1)
    weights = jnp.where(is_valid, jnp.exp(masked - local_peak[..., None]), 0.0)
    local_total = jnp.sum(weights, axis=-1)
    local_mixed = jnp.einsum("rgqs,rgsd->rgqd", weights, value_rows, precision=HIGHEST)

    def lane_row(values):
        row = jnp.concatenate(pieces_of(values.reshape(group_reqs, heads)), axis=1)
        return jnp.pad(row, ((0, 0), (0, head_size - row.shape[1])))[:, None, :]

    parts = jnp.concatenate(
        [
            local_mixed.reshape(group_reqs, heads, head_size).astype(BF16),
            lane_row(local_peak),
            lane_row(local_total),
            jnp.zeros((group_reqs, 2, head_size), BF16),
        ],
        axis=1,
    )
    gathered = swap(parts, "tp")
    tail = gathered[:, heads : heads + 2, : 3 * heads].astype(F32)
    tail = tail[..., :heads] + tail[..., heads : 2 * heads] + tail[..., 2 * heads :]
    peaks, totals = tail[:, 0], tail[:, 1]
    scale = jnp.exp(peaks - jnp.max(peaks, axis=0, keepdims=True))
    total = jnp.sum(scale * totals, axis=0)
    mixed = jnp.sum(scale[:, :, None] * gathered[:, :heads].astype(F32), axis=0)
    attention_row = (mixed / total[:, None]).astype(BF16)

    attention = spread(attention_row, "tp").reshape(group_reqs, width)
    projected = jnp.dot(attention, w_out, preferred_element_type=F32).astype(BF16)
    all_projected = spread(projected, "dp").reshape(total_reqs, projected.shape[1])
    home_ids = dp_group * group_reqs + jnp.arange(group_reqs, dtype=jnp.int32)
    at_home = choose_rows(home_ids[:, None] == placing[None, :], all_projected)
    proj_home = swap(at_home[:, None, :], "tp").reshape(1, width)
    hidden_dec = (resid_dec.astype(F32) + proj_home.astype(F32)).astype(BF16)

    route_weight = route_scale / jnp.sum(route_scale, axis=-1, keepdims=True)
    expert_ids = jnp.arange(experts, dtype=jnp.int32)
    hits = routes[:, :, None] == expert_ids[None, None, :]
    weight_of = jnp.sum(jnp.where(hits, route_weight[:, :, None], 0.0), axis=1)
    pre_rows = x_pre.shape[0]
    top_count = routes.shape[1]
    capacity = min(2 * (pre_rows + 1) * top_count // experts, pre_rows + 1)

    routed = jnp.any(hits[:pre_rows], axis=1)
    row_ids = jnp.arange(pre_rows, dtype=jnp.int32)
    before = (row_ids[None, :] < row_ids[:, None]).astype(BF16)
    position = jnp.dot(before, routed.astype(BF16), preferred_element_type=F32).astype(jnp.int32)
    slot_ids_e = jnp.arange(capacity, dtype=jnp.int32)
    pick = routed[:, :, None] & (position[:, :, None] == slot_ids_e[None, None, :])
    pick_table = pick.reshape(pre_rows, experts * capacity)
    x_f32 = x_pre.astype(F32)
    normed = rms(x_f32, moe_gain)
    outgoing = lax.dot_general(
        pick_table.astype(BF16), normed, (((0,), (0,)), ((), ())), preferred_element_type=F32
    ).astype(BF16)
    received = swap(outgoing.reshape(experts, capacity, width), "tp")
    expert_out = expert_units(received.reshape(experts * capacity, width), units)
    returned = swap(expert_out.reshape(experts, capacity, width), "tp")
    flat_back = returned.reshape(experts * capacity, width)
    high, middle, low = pieces_of(weight_of[:pre_rows])

    def mix(piece):
        table = jnp.where(pick, piece[:, :, None], jnp.zeros((), BF16))
        return jnp.dot(
            table.reshape(pre_rows, experts * capacity), flat_back, preferred_element_type=F32
        )

    out_pre = (x_f32 + (mix(high) + mix(middle) + mix(low))).astype(BF16)

    hidden_f32 = hidden_dec.astype(F32)
    normed_dec = rms(hidden_f32, moe_gain)
    group_rows = spread(normed_dec, "tp").reshape(group_reqs, width)
    dec_out = expert_units(group_rows, units)
    dec_back = swap(dec_out[:, None, :], "tp").reshape(experts, width)
    dec_weight = weight_of[pre_rows:]
    mixture = jnp.sum(dec_weight.reshape(experts, 1) * dec_back.astype(F32), axis=0, keepdims=True)
    out_dec = (hidden_f32 + mixture).astype(BF16)
    return (out_pre, out_dec)


def solution(mesh):
    placed = (
        P(("dp", "tp"), None),
        P(("dp", "tp"), None),
        P(("dp", "tp"), None),
        P(),
        P("dp"),
        P("dp"),
        P("dp", None, "tp", None),
        P("dp", None, "tp", None),
        P(None, "tp"),
        P(("dp", "tp"), None),
        P(("dp", "tp"), None),
        P(("dp", "tp"), None),
        P(),
        P("tp", "dp", None),
        P("tp", "dp", None),
        P("tp", "dp", None),
    )
    return jax.shard_map(
        on_device,
        mesh=mesh,
        in_specs=placed,
        out_specs=(P(("dp", "tp"), None), P(("dp", "tp"), None)),
        check_vma=False,
    )
```

```python
import jax
import jax.numpy as jnp
from jax import lax
from jax.sharding import PartitionSpec as P

HIGHEST = lax.Precision.HIGHEST
F32 = jnp.float32
BF16 = jnp.bfloat16


def contract_rows(left_rows, unit_rows):
    return lax.dot_general(
        left_rows, unit_rows, (((1,), (1,)), ((), ())), preferred_element_type=F32
    )


def swap(blocks, axis_name):
    return lax.all_to_all(blocks, axis_name, split_axis=0, concat_axis=0, tiled=True)


def spread(block, axis_name):
    members = lax.axis_size(axis_name)
    return swap(jnp.broadcast_to(block[None], (members,) + block.shape), axis_name)


def choose_rows(table, rows):
    return jnp.dot(table.astype(BF16), rows, preferred_element_type=F32).astype(BF16)


def pieces_of(x):
    high = lax.reduce_precision(x, 8, 7)
    middle = lax.reduce_precision(x - high, 8, 7)
    low = lax.reduce_precision(x - high - middle, 8, 7)
    return high.astype(BF16), middle.astype(BF16), low.astype(BF16)


def rms(rows_f32, gain):
    mean_square = jnp.mean(rows_f32 * rows_f32, axis=-1, keepdims=True)
    return (rows_f32 * lax.rsqrt(mean_square + 1e-06) * gain).astype(BF16)


def expert_units(rows, units):
    gate = contract_rows(rows, units[0])
    upper = contract_rows(rows, units[1])
    active = (jnp.maximum(gate, 0.0) * upper).astype(BF16)
    return jnp.dot(active, units[2], preferred_element_type=F32).astype(BF16)


def on_device(
    q_new,
    new_key_value,
    resid_dec,
    placing,
    lengths,
    write_pos,
    k_cache,
    value_cache,
    w_out,
    x_pre,
    routes,
    route_scale,
    moe_gain,
    w_gate,
    w_up,
    w_down,
):
    dp_size = lax.axis_size("dp")
    tp_size = lax.axis_size("tp")
    dp_group = lax.axis_index("dp")
    tp_lane = lax.axis_index("tp")
    group_reqs, kv_heads, slot_dev, head_size = k_cache.shape
    width = q_new.shape[1]
    heads = width // head_size
    per_group = heads // kv_heads
    total_reqs = placing.shape[0]
    experts = tp_size * w_gate.shape[0]
    assert group_reqs == tp_size and experts == tp_size

    out_rows = lax.all_gather(w_out.T, "tp", axis=0, tiled=True)
    stacked = jnp.concatenate([w_gate, w_up, w_down], axis=0)
    stacked, _ = lax.optimization_barrier((stacked, out_rows))
    units = lax.all_gather(stacked, "dp", axis=1, tiled=True)

    columns = heads + 2 * kv_heads
    share = tp_size // columns
    chosen_rows = group_reqs // share
    fresh = jnp.concatenate([q_new, new_key_value], axis=1).reshape(1, columns, 1, head_size)
    by_head = swap(
        jnp.broadcast_to(fresh, (share, columns, 1, head_size)).reshape(tp_size, 1, head_size), "tp"
    )
    all_rows = spread(by_head.reshape(tp_size, head_size), "dp").reshape(total_reqs, head_size)
    first_row = dp_group * group_reqs + (tp_lane // columns) * chosen_rows
    wanted = lax.dynamic_slice_in_dim(placing, first_row, chosen_rows)
    request_ids = jnp.arange(total_reqs, dtype=jnp.int32)
    mine = choose_rows(wanted[:, None] == request_ids[None, :], all_rows)
    heads_here = spread(mine, "tp").reshape(share, columns, chosen_rows, head_size)
    cached = jnp.transpose(heads_here, (0, 2, 1, 3)).reshape(group_reqs, columns, head_size)
    query_head_list = cached[:, :heads].reshape(group_reqs, kv_heads, per_group, head_size)
    incoming_key = cached[:, heads : heads + kv_heads][:, :, None, :]
    incoming_value = cached[:, heads + kv_heads :][:, :, None, :]

    slot_ids = tp_lane * slot_dev + jnp.arange(slot_dev, dtype=jnp.int32)
    written = (slot_ids[None, :] == write_pos[:, None])[:, None, :, None]
    key_rows = jnp.where(written, incoming_key, k_cache)
    value_rows = jnp.where(written, incoming_value, value_cache).astype(F32)
    scores = jnp.einsum(
        "rgqd,rgsd->rgqs", query_head_list, key_rows, preferred_element_type=F32
    ) * head_size ** (-0.5)
    is_valid = (slot_ids[None, :] < lengths[:, None])[:, None, None, :]
    masked = jnp.where(is_valid, scores, -1e30)
    local_peak = jnp.max(masked, axis=-1)
    weights = jnp.where(is_valid, jnp.exp(masked - local_peak[..., None]), 0.0)
    local_total = jnp.sum(weights, axis=-1)
    local_mixed = jnp.einsum("rgqs,rgsd->rgqd", weights, value_rows, precision=HIGHEST)

    def lane_row(values):
        row = jnp.concatenate(pieces_of(values.reshape(group_reqs, heads)), axis=1)
        return jnp.pad(row, ((0, 0), (0, head_size - row.shape[1])))[:, None, :]

    parts = jnp.concatenate(
        [
            local_mixed.reshape(group_reqs, heads, head_size).astype(BF16),
            lane_row(local_peak),
            lane_row(local_total),
            jnp.zeros((group_reqs, 2, head_size), BF16),
        ],
        axis=1,
    )
    gathered = swap(parts, "tp")
    tail = gathered[:, heads : heads + 2, : 3 * heads].astype(F32)
    tail = tail[..., :heads] + tail[..., heads : 2 * heads] + tail[..., 2 * heads :]
    peaks, totals = tail[:, 0], tail[:, 1]
    scale = jnp.exp(peaks - jnp.max(peaks, axis=0, keepdims=True))
    total = jnp.sum(scale * totals, axis=0)
    mixed = jnp.sum(scale[:, :, None] * gathered[:, :heads].astype(F32), axis=0)
    attention_row = (mixed / total[:, None]).astype(BF16)

    projected = contract_rows(attention_row.reshape(1, width), out_rows).astype(BF16)
    request = lax.dynamic_slice_in_dim(placing, dp_group * group_reqs + tp_lane, 1)[0]
    lane_of = jnp.arange(tp_size, dtype=jnp.int32) == request % tp_size
    no_value = jnp.zeros((), BF16)
    by_lane = swap(jnp.where(lane_of[:, None], projected, no_value).reshape(tp_size, heads, head_size), "tp")
    group_rows = lax.dynamic_slice_in_dim(placing, dp_group * group_reqs, group_reqs)
    here = group_rows % tp_size == tp_lane
    to_group = (group_rows // tp_size)[None, :] == jnp.arange(dp_size, dtype=jnp.int32)[:, None]
    outbound = choose_rows(to_group & here[None, :], by_lane.reshape(tp_size, width))
    inbound = swap(outbound.reshape(dp_size, heads, head_size), "dp").reshape(dp_size, width)
    home_ids = dp_group * tp_size + tp_lane
    source = jnp.sum(jnp.where(placing == home_ids, jnp.arange(total_reqs, dtype=jnp.int32), 0))
    source_group = source // group_reqs
    from_group = jnp.arange(dp_size, dtype=jnp.int32)[None, :] == source_group
    proj_home = choose_rows(from_group, inbound)
    hidden_dec = (resid_dec.astype(F32) + proj_home.astype(F32)).astype(BF16)

    route_weight = route_scale / jnp.sum(route_scale, axis=-1, keepdims=True)
    expert_ids = jnp.arange(experts, dtype=jnp.int32)
    hits = routes[:, :, None] == expert_ids[None, None, :]
    weight_of = jnp.sum(jnp.where(hits, route_weight[:, :, None], 0.0), axis=1)
    moe_rows = jnp.concatenate([x_pre, hidden_dec], axis=0)
    rows_dev = moe_rows.shape[0]
    top_count = routes.shape[1]
    capacity = min(2 * rows_dev * top_count // experts, rows_dev)
    routed = jnp.any(hits, axis=1)
    row_ids = jnp.arange(rows_dev, dtype=jnp.int32)
    before = (row_ids[None, :] < row_ids[:, None]).astype(BF16)
    position = jnp.dot(before, routed.astype(BF16), preferred_element_type=F32).astype(jnp.int32)
    slot_ids_e = jnp.arange(capacity, dtype=jnp.int32)
    pick = routed[:, :, None] & (position[:, :, None] == slot_ids_e[None, None, :])
    pick_table = pick.reshape(rows_dev, experts * capacity)
    rows_f32 = moe_rows.astype(F32)
    normed = rms(rows_f32, moe_gain)
    outgoing = lax.dot_general(
        pick_table.astype(BF16), normed, (((0,), (0,)), ((), ())), preferred_element_type=F32
    ).astype(BF16)
    received = swap(outgoing.reshape(experts, capacity, width), "tp")
    expert_out = expert_units(received.reshape(experts * capacity, width), units)
    returned = swap(expert_out.reshape(experts, capacity, width), "tp")
    flat_back = returned.reshape(experts * capacity, width)
    high, middle, low = pieces_of(weight_of)

    def mix(piece):
        table = jnp.where(pick, piece[:, :, None], no_value)
        return jnp.dot(
            table.reshape(rows_dev, experts * capacity), flat_back, preferred_element_type=F32
        )

    moe_out = (rows_f32 + (mix(high) + mix(middle) + mix(low))).astype(BF16)
    return (moe_out[: rows_dev - 1], moe_out[rows_dev - 1 :])


def solution(mesh):
    placed = (
        P(("dp", "tp"), None),
        P(("dp", "tp"), None),
        P(("dp", "tp"), None),
        P(),
        P("dp"),
        P("dp"),
        P("dp", None, "tp", None),
        P("dp", None, "tp", None),
        P(None, "tp"),
        P(("dp", "tp"), None),
        P(("dp", "tp"), None),
        P(("dp", "tp"), None),
        P(),
        P("tp", "dp", None),
        P("tp", "dp", None),
        P("tp", "dp", None),
    )
    return jax.shard_map(
        on_device,
        mesh=mesh,
        in_specs=placed,
        out_specs=(P(("dp", "tp"), None), P(("dp", "tp"), None)),
        check_vma=False,
    )
```

```python
import jax
import jax.numpy as jnp
from jax import lax
from jax.sharding import Mesh
from jax.sharding import PartitionSpec as P

TP = ("y", "x")
HIGHEST = lax.Precision.HIGHEST
F32 = jnp.float32
BF16 = jnp.bfloat16


def contract_rows(left_rows, unit_rows):
    return lax.dot_general(
        left_rows, unit_rows, (((1,), (1,)), ((), ())), preferred_element_type=F32
    )


def swap(blocks, axis_name):
    return lax.all_to_all(blocks, axis_name, split_axis=0, concat_axis=0, tiled=True)


def spread(block, axis_name):
    members = lax.axis_size(axis_name) if isinstance(axis_name, str) else lax.psum(1, axis_name)
    return swap(jnp.broadcast_to(block[None], (members,) + block.shape), axis_name)


def choose_rows(table, rows):
    return jnp.dot(table.astype(BF16), rows, preferred_element_type=F32).astype(BF16)


def pieces_of(x):
    high = lax.reduce_precision(x, 8, 7)
    middle = lax.reduce_precision(x - high, 8, 7)
    low = lax.reduce_precision(x - high - middle, 8, 7)
    return high.astype(BF16), middle.astype(BF16), low.astype(BF16)


def rms(rows_f32, gain):
    mean_square = jnp.mean(rows_f32 * rows_f32, axis=-1, keepdims=True)
    return (rows_f32 * lax.rsqrt(mean_square + 1e-06) * gain).astype(BF16)


def expert_units(rows, units):
    gate = contract_rows(rows, units[0])
    upper = contract_rows(rows, units[1])
    active = (jnp.maximum(gate, 0.0) * upper).astype(BF16)
    return jnp.dot(active, units[2], preferred_element_type=F32).astype(BF16)


def on_device(
    q_new,
    new_key_value,
    resid_dec,
    placing,
    lengths,
    write_pos,
    k_cache,
    value_cache,
    w_out,
    x_pre,
    routes,
    route_scale,
    moe_gain,
    w_gate,
    w_up,
    w_down,
):
    dp_size = lax.axis_size("dp")
    lines, posts = lax.axis_size("y"), lax.axis_size("x")
    tp_size = lines * posts
    dp_group = lax.axis_index("dp")
    line = lax.axis_index("y")
    tp_lane = line * posts + lax.axis_index("x")
    group_reqs, kv_heads, slot_dev, head_size = k_cache.shape
    width = q_new.shape[1]
    heads = width // head_size
    per_group = heads // kv_heads
    total_reqs = placing.shape[0]
    experts = tp_size * w_gate.shape[0]
    assert group_reqs == tp_size and experts == tp_size

    out_rows = lax.all_gather(w_out.T, "y", axis=0, tiled=True)
    units = lax.all_gather(
        jnp.concatenate([w_gate, w_up, w_down], axis=0), "dp", axis=1, tiled=True
    )

    no_value = jnp.zeros((), BF16)
    rows_dev, top_count = routes.shape
    pre_rows = rows_dev - 1
    capacity = min(2 * rows_dev * top_count // experts, rows_dev)
    route_weight = route_scale / jnp.sum(route_scale, axis=-1, keepdims=True)
    expert_ids = jnp.arange(experts, dtype=jnp.int32)
    hits = routes[:, :, None] == expert_ids[None, None, :]
    weight_of = jnp.sum(jnp.where(hits, route_weight[:, :, None], 0.0), axis=1)
    routed = jnp.any(hits, axis=1)

    row_ids = jnp.arange(rows_dev, dtype=jnp.int32)
    before = (row_ids[None, :] < row_ids[:, None]).astype(BF16)
    position = jnp.dot(before, routed.astype(BF16), preferred_element_type=F32).astype(jnp.int32)
    position = jnp.where(row_ids[:, None] == pre_rows, capacity - 1, position)
    slots = jnp.arange(capacity, dtype=jnp.int32)
    pick = routed[:, :, None] & (position[:, :, None] == slots[None, None, :])
    pick_table = pick.reshape(rows_dev, experts * capacity)
    x_f32 = x_pre.astype(F32)
    outgoing = lax.dot_general(
        pick_table[:pre_rows].astype(BF16),
        rms(x_f32, moe_gain),
        (((0,), (0,)), ((), ())),
        preferred_element_type=F32,
    ).astype(BF16)

    columns = heads + 2 * kv_heads
    share = tp_size // columns
    chosen_rows = group_reqs // share
    fresh = jnp.concatenate([q_new, new_key_value], axis=1).reshape(1, columns, 1, head_size)
    by_head = swap(
        jnp.broadcast_to(fresh, (share, columns, 1, head_size)).reshape(tp_size, 1, head_size), TP
    )
    by_head, outgoing = lax.optimization_barrier((by_head, outgoing))
    received = swap(outgoing.reshape(experts, capacity, width), TP)
    all_rows = lax.all_gather(by_head.reshape(tp_size, head_size), "dp", axis=0, tiled=True)
    first_row = dp_group * group_reqs + (tp_lane // columns) * chosen_rows
    wanted = lax.dynamic_slice_in_dim(placing, first_row, chosen_rows)
    request_ids = jnp.arange(total_reqs, dtype=jnp.int32)
    mine = choose_rows(wanted[:, None] == request_ids[None, :], all_rows)
    mine, received = lax.optimization_barrier((mine, received))
    heads_here = spread(mine, TP).reshape(share, columns, chosen_rows, head_size)
    cached = jnp.transpose(heads_here, (0, 2, 1, 3)).reshape(group_reqs, columns, head_size)
    query_head_list = cached[:, :heads].reshape(group_reqs, kv_heads, per_group, head_size)
    incoming_key = cached[:, heads : heads + kv_heads][:, :, None, :]
    incoming_value = cached[:, heads + kv_heads :][:, :, None, :]

    slot_ids = tp_lane * slot_dev + jnp.arange(slot_dev, dtype=jnp.int32)
    written = (slot_ids[None, :] == write_pos[:, None])[:, None, :, None]
    key_rows = jnp.where(written, incoming_key, k_cache)
    value_rows = jnp.where(written, incoming_value, value_cache).astype(F32)
    scores = jnp.einsum(
        "rgqd,rgsd->rgqs", query_head_list, key_rows, preferred_element_type=F32
    ) * head_size ** (-0.5)
    is_valid = (slot_ids[None, :] < lengths[:, None])[:, None, None, :]
    masked = jnp.where(is_valid, scores, -1e30)
    local_peak = jnp.max(masked, axis=-1)
    weights = jnp.where(is_valid, jnp.exp(masked - local_peak[..., None]), 0.0)
    local_total = jnp.sum(weights, axis=-1)
    local_mixed = jnp.einsum("rgqs,rgsd->rgqd", weights, value_rows, precision=HIGHEST)

    def lane_row(values):
        row = jnp.concatenate(pieces_of(values.reshape(group_reqs, heads)), axis=1)
        return jnp.pad(row, ((0, 0), (0, head_size - row.shape[1])))[:, None, :]

    parts = jnp.concatenate(
        [
            local_mixed.reshape(group_reqs, heads, head_size).astype(BF16),
            lane_row(local_peak),
            lane_row(local_total),
            jnp.zeros((group_reqs, 2, head_size), BF16),
        ],
        axis=1,
    )
    gathered = swap(parts, TP)
    tail = gathered[:, heads : heads + 2, : 3 * heads].astype(F32)
    tail = tail[..., :heads] + tail[..., heads : 2 * heads] + tail[..., 2 * heads :]
    peaks, totals = tail[:, 0], tail[:, 1]
    scale = jnp.exp(peaks - jnp.max(peaks, axis=0, keepdims=True))
    total = jnp.sum(scale * totals, axis=0)
    mixed = jnp.sum(scale[:, :, None] * gathered[:, :heads].astype(F32), axis=0)
    attention_row = (mixed / total[:, None]).astype(BF16)

    attention = spread(attention_row, "x").reshape(posts, width)
    projected = contract_rows(attention, out_rows).astype(BF16)
    post_columns = projected.shape[1]
    all_projected = spread(projected, "dp").reshape(dp_size * posts, post_columns)
    line_rows = placing.reshape(dp_size, lines, posts)
    line_rows = lax.dynamic_slice_in_dim(line_rows, line, 1, axis=1).reshape(1, dp_size * posts)
    home_ids = dp_group * group_reqs + jnp.arange(group_reqs, dtype=jnp.int32)
    at_home = choose_rows(home_ids[:, None] == line_rows, all_projected)
    from_lanes = swap(at_home.reshape(tp_size, post_columns // head_size, head_size), TP)
    from_lanes = from_lanes.reshape(lines, posts, post_columns).astype(F32)
    proj_home = jnp.sum(from_lanes, axis=0).reshape(posts, lines, post_columns // lines)
    proj_home = jnp.transpose(proj_home, (1, 0, 2)).reshape(1, width)
    hidden_f32 = (resid_dec.astype(F32) + proj_home).astype(BF16).astype(F32)

    pre_out = expert_units(received.reshape(experts * capacity, width), units)
    normed_dec = rms(hidden_f32, moe_gain)
    dec_rows = jnp.where(routed[pre_rows][:, None], normed_dec, no_value)
    group_rows = swap(dec_rows.reshape(experts, heads, head_size), TP).reshape(group_reqs, width)
    dec_out = expert_units(group_rows, units)
    last = (slots == capacity - 1)[None, :, None]
    pre_out = pre_out.reshape(experts, capacity, width)
    outbound = jnp.where(last, pre_out + dec_out[:, None, :], pre_out)
    returned = swap(outbound, TP)
    flat_back = returned.reshape(experts * capacity, width)
    high, middle, low = pieces_of(weight_of)

    def mix(piece):
        table = jnp.where(pick, piece[:, :, None], no_value)
        return jnp.dot(
            table.reshape(rows_dev, experts * capacity), flat_back, preferred_element_type=F32
        )

    mixture = mix(high) + mix(middle) + mix(low)
    out_pre = (x_f32 + mixture[:pre_rows]).astype(BF16)
    out_dec = (hidden_f32 + mixture[pre_rows:]).astype(BF16)
    return (out_pre, out_dec)


def solution(mesh):
    groups, lanes = mesh.devices.shape
    fine = Mesh(mesh.devices.reshape(groups, 8, lanes // 8), ("dp", "y", "x"))
    rows = P(("dp", "y", "x"), None)
    units = P(TP, "dp", None)
    cache = P("dp", None, TP, None)
    placed = (rows, rows, rows, P(), P("dp"), P("dp"), cache, cache, P(None, TP))
    placed = placed + (rows, rows, rows, P(), units, units, units)
    return jax.shard_map(
        on_device, mesh=fine, in_specs=placed, out_specs=(rows, rows), check_vma=False
    )
```

```python
import math

import jax
import jax.numpy as jnp
from jax import lax
from jax.sharding import Mesh
from jax.sharding import PartitionSpec as P

TP = ("y", "x")
HIGHEST = lax.Precision.HIGHEST
F32 = jnp.float32
BF16 = jnp.bfloat16


def contract_rows(left_rows, unit_rows):
    return lax.dot_general(
        left_rows, unit_rows, (((1,), (1,)), ((), ())), preferred_element_type=F32
    )


def swap(blocks, axis_name):
    return lax.all_to_all(blocks, axis_name, split_axis=0, concat_axis=0, tiled=True)


def spread(block, axis_name):
    members = lax.axis_size(axis_name) if isinstance(axis_name, str) else lax.psum(1, axis_name)
    return swap(jnp.broadcast_to(block[None], (members,) + block.shape), axis_name)


def choose_rows(table, rows):
    return jnp.dot(table.astype(BF16), rows, preferred_element_type=F32).astype(BF16)


def pieces_of(x):
    high = lax.reduce_precision(x, 8, 7)
    middle = lax.reduce_precision(x - high, 8, 7)
    low = lax.reduce_precision(x - high - middle, 8, 7)
    return high.astype(BF16), middle.astype(BF16), low.astype(BF16)


def rms(rows_f32, gain):
    mean_square = jnp.mean(rows_f32 * rows_f32, axis=-1, keepdims=True)
    return (rows_f32 * lax.rsqrt(mean_square + 1e-06) * gain).astype(BF16)


def expert_units(rows, units):
    gate = contract_rows(rows, units[0])
    upper = contract_rows(rows, units[1])
    active = (jnp.maximum(gate, 0.0) * upper).astype(BF16)
    return jnp.dot(active, units[2], preferred_element_type=F32).astype(BF16)


def on_device(
    q_new,
    new_key_value,
    resid_dec,
    placing,
    lengths,
    write_pos,
    k_cache,
    value_cache,
    w_out,
    x_pre,
    routes,
    route_scale,
    moe_gain,
    w_gate,
    w_up,
    w_down,
):
    dp_size = lax.axis_size("dp")
    lines, posts = lax.axis_size("y"), lax.axis_size("x")
    tp_size = lines * posts
    dp_group = lax.axis_index("dp")
    line = lax.axis_index("y")
    tp_lane = line * posts + lax.axis_index("x")
    group_reqs, kv_heads, slot_dev, head_size = k_cache.shape
    width = q_new.shape[1]
    heads = width // head_size
    per_group = heads // kv_heads
    total_reqs = placing.shape[0]
    experts = tp_size * w_gate.shape[0]
    assert group_reqs == tp_size and experts == tp_size

    turned = [
        (group * lines + other, (other + group // lines * lines) * lines + group % lines)
        for group in range(dp_size)
        for other in range(lines)
    ]
    line_columns = lax.ppermute(w_out.T, ("dp", "y"), turned)

    no_value = jnp.zeros((), BF16)
    rows_dev, top_count = routes.shape
    pre_rows = rows_dev - 1
    capacity = min(2 * rows_dev * top_count // experts, rows_dev)
    route_weight = route_scale / jnp.sum(route_scale, axis=-1, keepdims=True)
    expert_ids = jnp.arange(experts, dtype=jnp.int32)
    hits = routes[:, :, None] == expert_ids[None, None, :]
    weight_of = jnp.sum(jnp.where(hits, route_weight[:, :, None], 0.0), axis=1)

    routed = jnp.any(hits[:pre_rows], axis=1)
    row_ids = jnp.arange(pre_rows, dtype=jnp.int32)
    before = (row_ids[None, :] < row_ids[:, None]).astype(BF16)
    position = jnp.dot(before, routed.astype(BF16), preferred_element_type=F32).astype(jnp.int32)
    slots = jnp.arange(capacity, dtype=jnp.int32)
    pick = routed[:, :, None] & (position[:, :, None] == slots[None, None, :])
    pick_table = pick.reshape(pre_rows, experts * capacity)
    x_f32 = x_pre.astype(F32)
    outgoing = lax.dot_general(
        pick_table.astype(BF16),
        rms(x_f32, moe_gain),
        (((0,), (0,)), ((), ())),
        preferred_element_type=F32,
    ).astype(BF16)

    line_columns, outgoing = lax.optimization_barrier((line_columns, outgoing))
    units = lax.all_gather(
        jnp.concatenate([w_gate, w_up, w_down, line_columns[None]], axis=0),
        "dp",
        axis=1,
        tiled=True,
    )
    out_rows = units[3, : lines * w_out.shape[1]]

    columns = heads + 2 * kv_heads
    share = columns * head_size // posts
    post = lax.axis_index("x")
    fresh = jnp.concatenate([q_new, new_key_value], axis=1)
    fresh, outgoing = lax.optimization_barrier((fresh, outgoing))
    received = swap(outgoing.reshape(experts, capacity, width), TP)
    line_fresh = lax.all_gather(fresh, "x", axis=0, tiled=True)
    line_share = lax.dynamic_slice_in_dim(line_fresh, post * share, share, axis=1)
    all_rows = lax.all_gather(line_share, "dp", axis=0, tiled=True)
    wanted = lax.dynamic_slice_in_dim(placing, dp_group * group_reqs, group_reqs)
    held = jnp.arange(dp_size, dtype=jnp.int32)[:, None] * tp_size + line * posts
    held = (held + jnp.arange(posts, dtype=jnp.int32)[None, :]).reshape(1, dp_size * posts)
    mine = choose_rows(wanted[:, None] == held, all_rows)
    mine, received = lax.optimization_barrier((mine, received))
    chosen = jnp.sum(spread(mine, "y").astype(F32), axis=0).astype(BF16)
    cached = spread(chosen, "x").reshape(posts, group_reqs, columns // posts, head_size)
    cached = jnp.transpose(cached, (1, 0, 2, 3)).reshape(group_reqs, columns, head_size)
    query_head_list = cached[:, :heads].reshape(group_reqs, kv_heads, per_group, head_size)
    incoming_key = cached[:, heads : heads + kv_heads][:, :, None, :]
    incoming_value = cached[:, heads + kv_heads :][:, :, None, :]

    slot_ids = tp_lane * slot_dev + jnp.arange(slot_dev, dtype=jnp.int32)
    written = (slot_ids[None, :] == write_pos[:, None])[:, None, :, None]
    key_rows = jnp.where(written, incoming_key, k_cache)
    value_rows = jnp.where(written, incoming_value, value_cache).astype(F32)
    scores = jnp.einsum(
        "rgqd,rgsd->rgqs", query_head_list, key_rows, preferred_element_type=F32
    ) * head_size ** (-0.5)
    is_valid = (slot_ids[None, :] < lengths[:, None])[:, None, None, :]
    masked = jnp.where(is_valid, scores, -1e30)
    local_peak = jnp.max(masked, axis=-1)
    weights = jnp.where(is_valid, jnp.exp(masked - local_peak[..., None]), 0.0)
    local_total = jnp.sum(weights, axis=-1)
    local_mixed = jnp.einsum("rgqs,rgsd->rgqd", weights, value_rows, precision=HIGHEST)

    def lane_row(values):
        row = jnp.concatenate(pieces_of(values.reshape(group_reqs, heads)), axis=1)
        return jnp.pad(row, ((0, 0), (0, head_size - row.shape[1])))[:, None, :]

    parts = jnp.concatenate(
        [
            local_mixed.reshape(group_reqs, heads, head_size).astype(BF16),
            lane_row(local_peak),
            lane_row(local_total),
            jnp.zeros((group_reqs, 2, head_size), BF16),
        ],
        axis=1,
    )
    gathered = swap(parts, TP)

    pre_out = expert_units(received.reshape(experts * capacity, width), units)
    gathered, pre_out = lax.optimization_barrier((gathered, pre_out))
    returned = swap(pre_out.reshape(experts, capacity, width), TP)

    tail = gathered[:, heads : heads + 2, : 3 * heads].astype(F32)
    tail = tail[..., :heads] + tail[..., heads : 2 * heads] + tail[..., 2 * heads :]
    peaks, totals = tail[:, 0], tail[:, 1]
    scale = jnp.exp(peaks - jnp.max(peaks, axis=0, keepdims=True))
    total = jnp.sum(scale * totals, axis=0)
    mixed = jnp.sum(scale[:, :, None] * gathered[:, :heads].astype(F32), axis=0)
    attention_row = (mixed / total[:, None]).astype(BF16)

    attention = lax.all_gather(attention_row.reshape(1, width), "x", axis=0, tiled=True)
    projected = contract_rows(attention, out_rows).astype(BF16)
    post_columns = projected.shape[1]
    all_projected = lax.all_gather(projected, "dp", axis=0, tiled=True)
    line_rows = placing.reshape(dp_size, lines, posts)
    line_rows = lax.dynamic_slice_in_dim(line_rows, line, 1, axis=1).reshape(1, dp_size * posts)
    home_ids = dp_group * group_reqs + jnp.arange(group_reqs, dtype=jnp.int32)
    at_home = choose_rows(home_ids[:, None] == line_rows, all_projected)
    at_home, returned = lax.optimization_barrier((at_home, returned))
    from_lanes = swap(at_home.reshape(tp_size, -1, math.gcd(post_columns, head_size)), TP)
    from_lanes = from_lanes.reshape(lines, posts, post_columns).astype(F32)
    proj_home = jnp.sum(from_lanes, axis=0).reshape(posts, lines, post_columns // lines)
    proj_home = jnp.transpose(proj_home, (1, 0, 2)).reshape(1, width)
    hidden_f32 = (resid_dec.astype(F32) + proj_home).astype(BF16).astype(F32)

    normed_dec = rms(hidden_f32, moe_gain)
    group_rows = spread(normed_dec.reshape(heads, head_size), TP).reshape(group_reqs, width)
    dec_out = expert_units(group_rows, units)
    dec_back = swap(dec_out.reshape(group_reqs, heads, head_size), TP).astype(F32)
    dec_weight = weight_of[pre_rows:].reshape(experts, 1, 1)
    dec_mixture = jnp.sum(dec_weight * dec_back, axis=0).reshape(1, width)
    out_dec = (hidden_f32 + dec_mixture).astype(BF16)

    flat_back = returned.reshape(experts * capacity, width)
    high, middle, low = pieces_of(weight_of[:pre_rows])

    def mix(piece):
        table = jnp.where(pick, piece[:, :, None], no_value)
        return jnp.dot(
            table.reshape(pre_rows, experts * capacity), flat_back, preferred_element_type=F32
        )

    out_pre = (x_f32 + (mix(high) + mix(middle) + mix(low))).astype(BF16)
    return (out_pre, out_dec)


def solution(mesh):
    groups, lanes = mesh.devices.shape
    lines = min(8, groups)
    fine = Mesh(mesh.devices.reshape(groups, lines, lanes // lines), ("dp", "y", "x"))
    rows = P(("dp", "y", "x"), None)
    units = P(TP, "dp", None)
    cache = P("dp", None, TP, None)
    placed = (rows, rows, rows, P(), P("dp"), P("dp"), cache, cache, P(None, TP))
    placed = placed + (rows, rows, rows, P(), units, units, units)
    return jax.shard_map(
        on_device, mesh=fine, in_specs=placed, out_specs=(rows, rows), check_vma=False
    )
```

```python
import jax
import jax.numpy as jnp
from jax import lax
from jax.sharding import Mesh
from jax.sharding import PartitionSpec as P

TP = ("y", "x")
HIGHEST = lax.Precision.HIGHEST
F32 = jnp.float32
BF16 = jnp.bfloat16


def contract_rows(left_rows, unit_rows):
    return lax.dot_general(
        left_rows, unit_rows, (((1,), (1,)), ((), ())), preferred_element_type=F32
    )


def swap(blocks, axis_name):
    return lax.all_to_all(blocks, axis_name, split_axis=0, concat_axis=0, tiled=True)


def spread(block, axis_name):
    members = lax.axis_size(axis_name) if isinstance(axis_name, str) else lax.psum(1, axis_name)
    return swap(jnp.broadcast_to(block[None], (members,) + block.shape), axis_name)


def choose_rows(table, rows):
    return jnp.dot(table.astype(BF16), rows, preferred_element_type=F32).astype(BF16)


def pieces_of(x):
    high = lax.reduce_precision(x, 8, 7)
    middle = lax.reduce_precision(x - high, 8, 7)
    low = lax.reduce_precision(x - high - middle, 8, 7)
    return high.astype(BF16), middle.astype(BF16), low.astype(BF16)


def rms(rows_f32, gain):
    mean_square = jnp.mean(rows_f32 * rows_f32, axis=-1, keepdims=True)
    return (rows_f32 * lax.rsqrt(mean_square + 1e-06) * gain).astype(BF16)


def expert_units(rows, units):
    gate = contract_rows(rows, units[0])
    upper = contract_rows(rows, units[1])
    active = (jnp.maximum(gate, 0.0) * upper).astype(BF16)
    return jnp.dot(active, units[2], preferred_element_type=F32).astype(BF16)


def on_device(
    q_new,
    new_key_value,
    resid_dec,
    placing,
    lengths,
    write_pos,
    k_cache,
    value_cache,
    w_out,
    x_pre,
    routes,
    route_scale,
    moe_gain,
    w_gate,
    w_up,
    w_down,
):
    dp_size = lax.axis_size("dp")
    lines, posts = lax.axis_size("y"), lax.axis_size("x")
    tp_size = lines * posts
    dp_group = lax.axis_index("dp")
    line = lax.axis_index("y")
    tp_lane = line * posts + lax.axis_index("x")
    group_reqs, kv_heads, slot_dev, head_size = k_cache.shape
    width = q_new.shape[1]
    heads = width // head_size
    per_group = heads // kv_heads
    total_reqs = placing.shape[0]
    experts = tp_size * w_gate.shape[0]
    assert group_reqs == tp_size and experts == tp_size

    turned = []
    for group in range(dp_size):
        for lane in range(tp_size):
            taker = lane % lines + group // lines * lines
            place = (taker * lines + group % lines) * posts + lane // lines
            turned.append((group * tp_size + lane, place))
    post_part = lax.ppermute(w_out.T, ("dp", "y", "x"), turned)

    no_value = jnp.zeros((), BF16)
    rows_dev, top_count = routes.shape
    pre_rows = rows_dev - 1
    capacity = min(2 * rows_dev * top_count // experts, rows_dev)
    route_weight = route_scale / jnp.sum(route_scale, axis=-1, keepdims=True)
    expert_ids = jnp.arange(experts, dtype=jnp.int32)
    hits = routes[:, :, None] == expert_ids[None, None, :]
    weight_of = jnp.sum(jnp.where(hits, route_weight[:, :, None], 0.0), axis=1)

    routed = jnp.any(hits[:pre_rows], axis=1)
    row_ids = jnp.arange(pre_rows, dtype=jnp.int32)
    before = (row_ids[None, :] < row_ids[:, None]).astype(BF16)
    position = jnp.dot(before, routed.astype(BF16), preferred_element_type=F32).astype(jnp.int32)
    slots = jnp.arange(capacity, dtype=jnp.int32)
    pick = routed[:, :, None] & (position[:, :, None] == slots[None, None, :])
    pick_table = pick.reshape(pre_rows, experts * capacity)
    x_f32 = x_pre.astype(F32)
    outgoing = lax.dot_general(
        pick_table.astype(BF16),
        rms(x_f32, moe_gain),
        (((0,), (0,)), ((), ())),
        preferred_element_type=F32,
    ).astype(BF16)

    post_part, outgoing = lax.optimization_barrier((post_part, outgoing))
    units = lax.all_gather(
        jnp.concatenate([w_gate, w_up, w_down, post_part[None]], axis=0),
        "dp",
        axis=1,
        tiled=True,
    )
    out_rows = units[3, : lines * w_out.shape[1]]

    columns = heads + 2 * kv_heads
    share = columns * head_size // posts
    post = lax.axis_index("x")
    fresh = jnp.concatenate([q_new, new_key_value, resid_dec], axis=1)
    fresh, outgoing = lax.optimization_barrier((fresh, outgoing))
    received = swap(outgoing.reshape(experts, capacity, width), TP)
    line_fresh = lax.all_gather(fresh, "x", axis=0, tiled=True)
    line_share = lax.dynamic_slice_in_dim(line_fresh, post * share, share, axis=1)
    post_columns = width // posts
    line_resid = lax.dynamic_slice_in_dim(
        line_fresh, columns * head_size + post * post_columns, post_columns, axis=1
    )
    all_rows = lax.all_gather(line_share, "dp", axis=0, tiled=True)
    wanted = lax.dynamic_slice_in_dim(placing, dp_group * group_reqs, group_reqs)
    held = jnp.arange(dp_size, dtype=jnp.int32)[:, None] * tp_size + line * posts
    held = (held + jnp.arange(posts, dtype=jnp.int32)[None, :]).reshape(1, dp_size * posts)
    mine = choose_rows(wanted[:, None] == held, all_rows)
    mine, received = lax.optimization_barrier((mine, received))
    chosen = jnp.sum(spread(mine, "y").astype(F32), axis=0).astype(BF16)
    cached = spread(chosen, "x").reshape(posts, group_reqs, columns // posts, head_size)
    cached = jnp.transpose(cached, (1, 0, 2, 3)).reshape(group_reqs, columns, head_size)
    query_head_list = cached[:, :heads].reshape(group_reqs, kv_heads, per_group, head_size)
    incoming_key = cached[:, heads : heads + kv_heads][:, :, None, :]
    incoming_value = cached[:, heads + kv_heads :][:, :, None, :]

    slot_ids = tp_lane * slot_dev + jnp.arange(slot_dev, dtype=jnp.int32)
    written = (slot_ids[None, :] == write_pos[:, None])[:, None, :, None]
    key_rows = jnp.where(written, incoming_key, k_cache)
    value_rows = jnp.where(written, incoming_value, value_cache).astype(F32)
    scores = jnp.einsum(
        "rgqd,rgsd->rgqs", query_head_list, key_rows, preferred_element_type=F32
    ) * head_size ** (-0.5)
    is_valid = (slot_ids[None, :] < lengths[:, None])[:, None, None, :]
    masked = jnp.where(is_valid, scores, -1e30)
    local_peak = jnp.max(masked, axis=-1)
    weights = jnp.where(is_valid, jnp.exp(masked - local_peak[..., None]), 0.0)
    local_total = jnp.sum(weights, axis=-1)
    local_mixed = jnp.einsum("rgqs,rgsd->rgqd", weights, value_rows, precision=HIGHEST)

    def lane_row(values):
        row = jnp.concatenate(pieces_of(values.reshape(group_reqs, heads)), axis=1)
        return jnp.pad(row, ((0, 0), (0, head_size - row.shape[1])))[:, None, :]

    parts = jnp.concatenate(
        [
            local_mixed.reshape(group_reqs, heads, head_size).astype(BF16),
            lane_row(local_peak),
            lane_row(local_total),
            jnp.zeros((group_reqs, 2, head_size), BF16),
        ],
        axis=1,
    )
    gathered = swap(parts, TP)

    pre_out = expert_units(received.reshape(experts * capacity, width), units)
    gathered, pre_out = lax.optimization_barrier((gathered, pre_out))
    returned = swap(pre_out.reshape(experts, capacity, width), TP)

    tail = gathered[:, heads : heads + 2, : 3 * heads].astype(F32)
    tail = tail[..., :heads] + tail[..., heads : 2 * heads] + tail[..., 2 * heads :]
    peaks, totals = tail[:, 0], tail[:, 1]
    scale = jnp.exp(peaks - jnp.max(peaks, axis=0, keepdims=True))
    total = jnp.sum(scale * totals, axis=0)
    mixed = jnp.sum(scale[:, :, None] * gathered[:, :heads].astype(F32), axis=0)
    attention_row = (mixed / total[:, None]).astype(BF16)

    attention = lax.all_gather(attention_row.reshape(1, width), "x", axis=0, tiled=True)
    projected = contract_rows(attention, out_rows).astype(BF16)
    all_projected = lax.all_gather(projected, "dp", axis=0, tiled=True)
    line_rows = placing.reshape(dp_size, lines, posts)
    line_rows = lax.dynamic_slice_in_dim(line_rows, line, 1, axis=1).reshape(1, dp_size * posts)
    lane_ids = jnp.arange(group_reqs, dtype=jnp.int32)[:, None]
    from_cache = (dp_group * group_reqs + lane_ids == line_rows).astype(BF16)
    from_line = lane_ids == line * posts + jnp.arange(posts, dtype=jnp.int32)[None, :]
    at_home = jnp.dot(from_cache, all_projected, preferred_element_type=F32)
    at_home = at_home + jnp.dot(from_line.astype(BF16), line_resid, preferred_element_type=F32)
    at_home = at_home.astype(BF16)
    at_home, returned = lax.optimization_barrier((at_home, returned))
    hidden_share = jnp.sum(spread(at_home, "y").astype(F32), axis=0).astype(BF16)
    hidden_all = jnp.transpose(spread(hidden_share, "x"), (1, 0, 2)).reshape(group_reqs, width)
    hidden_f32 = lax.dynamic_slice_in_dim(hidden_all, tp_lane, 1).astype(F32)

    dec_out = expert_units(rms(hidden_all.astype(F32), moe_gain), units)
    dec_back = swap(dec_out.reshape(group_reqs, heads, head_size), TP).astype(F32)
    dec_weight = weight_of[pre_rows:].reshape(experts, 1, 1)
    dec_mixture = jnp.sum(dec_weight * dec_back, axis=0).reshape(1, width)
    out_dec = (hidden_f32 + dec_mixture).astype(BF16)

    flat_back = returned.reshape(experts * capacity, width)
    high, middle, low = pieces_of(weight_of[:pre_rows])

    def mix(piece):
        table = jnp.where(pick, piece[:, :, None], no_value)
        return jnp.dot(
            table.reshape(pre_rows, experts * capacity), flat_back, preferred_element_type=F32
        )

    out_pre = (x_f32 + (mix(high) + mix(middle) + mix(low))).astype(BF16)
    return (out_pre, out_dec)


def solution(mesh):
    groups, lanes = mesh.devices.shape
    lines = min(8, groups)
    fine = Mesh(mesh.devices.reshape(groups, lines, lanes // lines), ("dp", "y", "x"))
    rows = P(("dp", "y", "x"), None)
    units = P(TP, "dp", None)
    cache = P("dp", None, TP, None)
    placed = (rows, rows, rows, P(), P("dp"), P("dp"), cache, cache, P(None, TP))
    placed = placed + (rows, rows, rows, P(), units, units, units)
    return jax.shard_map(
        on_device, mesh=fine, in_specs=placed, out_specs=(rows, rows), check_vma=False
    )
```

```python
import jax
import jax.numpy as jnp
from jax import lax
from jax.sharding import Mesh
from jax.sharding import PartitionSpec as P

TP = ("y", "x")
F32 = jnp.float32
BF16 = jnp.bfloat16


def contract_rows(left_rows, unit_rows):
    return lax.dot_general(
        left_rows, unit_rows, (((1,), (1,)), ((), ())), preferred_element_type=F32
    )


def swap(blocks, axis_name):
    return lax.all_to_all(blocks, axis_name, split_axis=0, concat_axis=0, tiled=True)


def spread(block, axis_name):
    members = lax.axis_size(axis_name) if isinstance(axis_name, str) else lax.psum(1, axis_name)
    return swap(jnp.broadcast_to(block[None], (members,) + block.shape), axis_name)


def choose_rows(table, rows):
    return jnp.dot(table.astype(BF16), rows, preferred_element_type=F32).astype(BF16)


def pieces_of(x):
    high = lax.reduce_precision(x, 8, 7)
    middle = lax.reduce_precision(x - high, 8, 7)
    low = lax.reduce_precision(x - high - middle, 8, 7)
    return high.astype(BF16), middle.astype(BF16), low.astype(BF16)


def rms(rows_f32, gain):
    mean_square = jnp.mean(rows_f32 * rows_f32, axis=-1, keepdims=True)
    return (rows_f32 * lax.rsqrt(mean_square + 1e-06) * gain).astype(BF16)


def expert_units(rows, units, joined=False):
    if joined:
        both = contract_rows(rows, units[:2].reshape(-1, units.shape[2]))
        gate, upper = both[:, : units.shape[1]], both[:, units.shape[1] :]
    else:
        gate = contract_rows(rows, units[0])
        upper = contract_rows(rows, units[1])
    active = (jnp.maximum(gate, 0.0) * upper).astype(BF16)
    return jnp.dot(active, units[2], preferred_element_type=F32).astype(BF16)


def on_device(
    q_new,
    new_key_value,
    resid_dec,
    placing,
    lengths,
    write_pos,
    k_cache,
    value_cache,
    w_out,
    x_pre,
    routes,
    route_scale,
    moe_gain,
    w_gate,
    w_up,
    w_down,
):
    dp_size = lax.axis_size("dp")
    lines, posts = lax.axis_size("y"), lax.axis_size("x")
    tp_size = lines * posts
    dp_group = lax.axis_index("dp")
    line = lax.axis_index("y")
    tp_lane = line * posts + lax.axis_index("x")
    group_reqs, kv_heads, slot_dev, head_size = k_cache.shape
    width = q_new.shape[1]
    heads = width // head_size
    per_group = heads // kv_heads
    total_reqs = placing.shape[0]
    experts = tp_size * w_gate.shape[0]
    assert group_reqs == tp_size and experts == tp_size

    turned = []
    for group in range(dp_size):
        for lane in range(tp_size):
            taker = lane % lines + group // lines * lines
            place = (taker * lines + group % lines) * posts + lane // lines
            turned.append((group * tp_size + lane, place))
    post_part = lax.ppermute(w_out.T, ("dp", "y", "x"), turned)

    no_value = jnp.zeros((), BF16)
    rows_dev, top_count = routes.shape
    pre_rows = rows_dev - 1
    capacity = min(2 * rows_dev * top_count // experts, rows_dev)
    route_weight = route_scale / jnp.sum(route_scale, axis=-1, keepdims=True)
    expert_ids = jnp.arange(experts, dtype=jnp.int32)
    hits = routes[:, :, None] == expert_ids[None, None, :]
    weight_of = jnp.sum(jnp.where(hits, route_weight[:, :, None], 0.0), axis=1)

    routed = jnp.any(hits[:pre_rows], axis=1)
    row_ids = jnp.arange(pre_rows, dtype=jnp.int32)
    before = (row_ids[None, :] < row_ids[:, None]).astype(BF16)
    position = jnp.dot(before, routed.astype(BF16), preferred_element_type=F32).astype(jnp.int32)
    slots = jnp.arange(capacity, dtype=jnp.int32)
    pick = routed[:, :, None] & (position[:, :, None] == slots[None, None, :])
    pick_table = pick.reshape(pre_rows, experts * capacity)
    x_f32 = x_pre.astype(F32)
    outgoing = lax.dot_general(
        pick_table.astype(BF16),
        rms(x_f32, moe_gain),
        (((0,), (0,)), ((), ())),
        preferred_element_type=F32,
    ).astype(BF16)

    post_part, outgoing = lax.optimization_barrier((post_part, outgoing))
    units = lax.all_gather(
        jnp.concatenate([w_gate, w_up, w_down, post_part[None]], axis=0),
        "dp",
        axis=1,
        tiled=True,
    )
    out_rows = units[3, : lines * w_out.shape[1]]

    columns = heads + 2 * kv_heads
    share = columns * head_size // posts
    post = lax.axis_index("x")
    fresh = jnp.concatenate([q_new, new_key_value, resid_dec], axis=1)
    fresh, outgoing = lax.optimization_barrier((fresh, outgoing))
    received = swap(outgoing.reshape(experts, capacity, width), TP)
    line_fresh = lax.all_gather(fresh, "x", axis=0, tiled=True)
    line_share = lax.dynamic_slice_in_dim(line_fresh, post * share, share, axis=1)
    post_columns = width // posts
    line_resid = lax.dynamic_slice_in_dim(
        line_fresh, columns * head_size + post * post_columns, post_columns, axis=1
    )
    all_rows = lax.all_gather(line_share, "dp", axis=0, tiled=True)
    wanted = lax.dynamic_slice_in_dim(placing, dp_group * group_reqs, group_reqs)
    held = jnp.arange(dp_size, dtype=jnp.int32)[:, None] * tp_size + line * posts
    held = (held + jnp.arange(posts, dtype=jnp.int32)[None, :]).reshape(1, dp_size * posts)
    mine = choose_rows(jnp.tile(wanted, lines)[:, None] == held, all_rows)
    mine, received = lax.optimization_barrier((mine, received))
    chosen = jnp.sum(swap(mine.reshape(lines, group_reqs, share), "y").astype(F32), axis=0).astype(BF16)
    cached = spread(chosen, "x").reshape(posts, group_reqs, columns // posts, head_size)
    cached = jnp.transpose(cached, (1, 0, 2, 3)).reshape(group_reqs, columns, head_size)
    query_head_list = cached[:, :heads].reshape(group_reqs, kv_heads, per_group, head_size)
    incoming_key = cached[:, heads : heads + kv_heads][:, :, None, :]
    incoming_value = cached[:, heads + kv_heads :][:, :, None, :]

    slot_ids = tp_lane * slot_dev + jnp.arange(slot_dev, dtype=jnp.int32)
    written = (slot_ids[None, :] == write_pos[:, None])[:, None, :, None]
    key_rows = jnp.where(written, incoming_key, k_cache)
    value_rows = jnp.where(written, incoming_value, value_cache)
    scores = jnp.einsum(
        "rgqd,rgsd->rgqs", query_head_list, key_rows, preferred_element_type=F32
    ) * head_size ** (-0.5)
    is_valid = (slot_ids[None, :] < lengths[:, None])[:, None, None, :]
    masked = jnp.where(is_valid, scores, -1e30)
    local_peak = jnp.max(masked, axis=-1)
    weights = jnp.where(is_valid, jnp.exp(masked - local_peak[..., None]), 0.0)
    local_total = jnp.sum(weights, axis=-1)
    high = lax.reduce_precision(weights, 8, 7)
    halves = jnp.concatenate([high, weights - high], axis=2).astype(BF16)
    local_mixed = jnp.einsum(
        "rgqs,rgsd->rgqd", halves, value_rows, preferred_element_type=F32
    )
    local_mixed = local_mixed[:, :, :per_group] + local_mixed[:, :, per_group:]

    def lane_row(values):
        row = jnp.concatenate(pieces_of(values.reshape(group_reqs, heads)), axis=1)
        return jnp.pad(row, ((0, 0), (0, head_size - row.shape[1])))[:, None, :]

    parts = jnp.concatenate(
        [
            local_mixed.reshape(group_reqs, heads, head_size).astype(BF16),
            lane_row(local_peak),
            lane_row(local_total),
            jnp.zeros((group_reqs, 2, head_size), BF16),
        ],
        axis=1,
    )
    gathered = swap(parts, TP)

    pre_out = expert_units(received.reshape(experts * capacity, width), units)
    gathered, pre_out = lax.optimization_barrier((gathered, pre_out))
    returned = swap(pre_out.reshape(experts, capacity, width), TP)

    tail = gathered[:, heads : heads + 2, : 3 * heads].astype(F32)
    tail = tail[..., :heads] + tail[..., heads : 2 * heads] + tail[..., 2 * heads :]
    peaks, totals = tail[:, 0], tail[:, 1]
    scale = jnp.exp(peaks - jnp.max(peaks, axis=0, keepdims=True))
    total = jnp.sum(scale * totals, axis=0)
    mixed = jnp.sum(scale[:, :, None] * gathered[:, :heads].astype(F32), axis=0)
    attention_row = (mixed / total[:, None]).astype(BF16)

    attention = lax.all_gather(attention_row.reshape(1, width), "x", axis=0, tiled=True)
    projected = contract_rows(attention, out_rows).astype(BF16)
    all_projected = lax.all_gather(projected, "dp", axis=0, tiled=True)
    line_rows = placing.reshape(dp_size, lines, posts)
    line_rows = lax.dynamic_slice_in_dim(line_rows, line, 1, axis=1).reshape(1, dp_size * posts)
    lane_ids = jnp.tile(jnp.arange(group_reqs, dtype=jnp.int32), lines)[:, None]
    from_cache = (dp_group * group_reqs + lane_ids == line_rows).astype(BF16)
    from_line = lane_ids == line * posts + jnp.arange(posts, dtype=jnp.int32)[None, :]
    at_home = jnp.dot(from_cache, all_projected, preferred_element_type=F32)
    at_home = at_home + jnp.dot(from_line.astype(BF16), line_resid, preferred_element_type=F32)
    at_home = at_home.astype(BF16)
    at_home, returned = lax.optimization_barrier((at_home, returned))
    at_home = swap(at_home.reshape(lines, group_reqs, post_columns), "y")
    hidden_share = jnp.sum(at_home.astype(F32), axis=0).astype(BF16)
    hidden_all = jnp.transpose(spread(hidden_share, "x"), (1, 0, 2)).reshape(group_reqs, width)
    hidden_f32 = lax.dynamic_slice_in_dim(hidden_all, tp_lane, 1).astype(F32)

    dec_out = expert_units(rms(hidden_all.astype(F32), moe_gain), units, joined=True)
    dec_back = swap(dec_out.reshape(group_reqs, heads, head_size), TP).astype(F32)
    dec_weight = weight_of[pre_rows:].reshape(experts, 1, 1)
    dec_mixture = jnp.sum(dec_weight * dec_back, axis=0).reshape(1, width)
    out_dec = (hidden_f32 + dec_mixture).astype(BF16)

    flat_back = returned.reshape(experts * capacity, width)
    high, middle, low = pieces_of(weight_of[:pre_rows])

    def mix(piece):
        table = jnp.where(pick, piece[:, :, None], no_value)
        return jnp.dot(
            table.reshape(pre_rows, experts * capacity), flat_back, preferred_element_type=F32
        )

    out_pre = (x_f32 + (mix(high) + mix(middle) + mix(low))).astype(BF16)
    return (out_pre, out_dec)


def solution(mesh):
    groups, lanes = mesh.devices.shape
    lines = min(8, groups)
    fine = Mesh(mesh.devices.reshape(groups, lines, lanes // lines), ("dp", "y", "x"))
    rows = P(("dp", "y", "x"), None)
    units = P(TP, "dp", None)
    cache = P("dp", None, TP, None)
    placed = (rows, rows, rows, P(), P("dp"), P("dp"), cache, cache, P(None, TP))
    placed = placed + (rows, rows, rows, P(), units, units, units)
    return jax.shard_map(
        on_device, mesh=fine, in_specs=placed, out_specs=(rows, rows), check_vma=False
    )
```

```python
import jax
import jax.numpy as jnp
from jax import lax
from jax.sharding import Mesh
from jax.sharding import PartitionSpec as P

TP = ("y", "x")
F32 = jnp.float32
BF16 = jnp.bfloat16


def contract_rows(left_rows, unit_rows):
    return lax.dot_general(
        left_rows, unit_rows, (((1,), (1,)), ((), ())), preferred_element_type=F32
    )


def swap(blocks, axis_name):
    return lax.all_to_all(blocks, axis_name, split_axis=0, concat_axis=0, tiled=True)


def choose_rows(table, rows):
    return jnp.dot(table.astype(BF16), rows, preferred_element_type=F32).astype(BF16)


def pieces_of(x):
    high = lax.reduce_precision(x, 8, 7)
    middle = lax.reduce_precision(x - high, 8, 7)
    low = lax.reduce_precision(x - high - middle, 8, 7)
    return high.astype(BF16), middle.astype(BF16), low.astype(BF16)


def rms(rows_f32, gain):
    mean_square = jnp.mean(rows_f32 * rows_f32, axis=-1, keepdims=True)
    return (rows_f32 * lax.rsqrt(mean_square + 1e-06) * gain).astype(BF16)


def sum_and_copy(parts, copies):
    count, rows, columns = parts.shape
    same = jnp.arange(copies * rows, dtype=jnp.int32)[:, None] % rows
    same = same == jnp.arange(count * rows, dtype=jnp.int32)[None, :] % rows
    return choose_rows(same, parts.reshape(count * rows, columns)).reshape(copies, rows, columns)


def expert_units(rows, units):
    gate = contract_rows(rows, units[0])
    upper = contract_rows(rows, units[1])
    active = (jnp.maximum(gate, 0.0) * upper).astype(BF16)
    return jnp.dot(active, units[2], preferred_element_type=F32).astype(BF16)


def on_device(
    q_new,
    new_key_value,
    resid_dec,
    placing,
    lengths,
    write_pos,
    k_cache,
    value_cache,
    w_out,
    x_pre,
    routes,
    route_scale,
    moe_gain,
    w_gate,
    w_up,
    w_down,
):
    dp_size = lax.axis_size("dp")
    lines, posts = lax.axis_size("y"), lax.axis_size("x")
    tp_size = lines * posts
    dp_group = lax.axis_index("dp")
    line = lax.axis_index("y")
    tp_lane = line * posts + lax.axis_index("x")
    group_reqs, kv_heads, slot_dev, head_size = k_cache.shape
    width = q_new.shape[1]
    heads = width // head_size
    per_group = heads // kv_heads
    total_reqs = placing.shape[0]
    experts = tp_size * w_gate.shape[0]
    assert group_reqs == tp_size and experts == tp_size

    turned = []
    for group in range(dp_size):
        for lane in range(tp_size):
            taker = lane % lines + group // lines * lines
            place = (taker * lines + group % lines) * posts + lane // lines
            turned.append((group * tp_size + lane, place))
    post_part = lax.ppermute(w_out.T, ("dp", "y", "x"), turned)

    no_value = jnp.zeros((), BF16)
    rows_dev, top_count = routes.shape
    pre_rows = rows_dev - 1
    capacity = min(2 * rows_dev * top_count // experts, rows_dev)
    route_weight = route_scale / jnp.sum(route_scale, axis=-1, keepdims=True)
    expert_ids = jnp.arange(experts, dtype=jnp.int32)
    hits = routes[:, :, None] == expert_ids[None, None, :]
    weight_of = jnp.sum(jnp.where(hits, route_weight[:, :, None], 0.0), axis=1)

    routed = jnp.any(hits[:pre_rows], axis=1)
    row_ids = jnp.arange(pre_rows, dtype=jnp.int32)
    before = (row_ids[None, :] < row_ids[:, None]).astype(BF16)
    position = jnp.dot(before, routed.astype(BF16), preferred_element_type=F32).astype(jnp.int32)
    slots = jnp.arange(capacity, dtype=jnp.int32)
    pick = routed[:, :, None] & (position[:, :, None] == slots[None, None, :])
    pick_table = pick.reshape(pre_rows, experts * capacity)
    x_f32 = x_pre.astype(F32)
    outgoing = lax.dot_general(
        pick_table.astype(BF16),
        lax.optimization_barrier(rms(x_f32, moe_gain)),
        (((0,), (0,)), ((), ())),
        preferred_element_type=F32,
    ).astype(BF16)

    post_part, outgoing = lax.optimization_barrier((post_part, outgoing))
    units = lax.all_gather(
        jnp.concatenate([w_gate, w_up, w_down, post_part[None]], axis=0),
        "dp",
        axis=1,
        tiled=True,
    )
    out_rows = units[3, : lines * w_out.shape[1]]

    columns = heads + 2 * kv_heads
    share = columns * head_size // posts
    post = lax.axis_index("x")
    fresh = jnp.concatenate([q_new, new_key_value, resid_dec], axis=1)
    fresh, outgoing = lax.optimization_barrier((fresh, outgoing))
    received = swap(outgoing.reshape(experts, capacity, width), TP)
    line_fresh = lax.all_gather(fresh, "x", axis=0, tiled=True)
    line_share = lax.dynamic_slice_in_dim(line_fresh, post * share, share, axis=1)
    post_columns = width // posts
    line_resid = lax.dynamic_slice_in_dim(
        line_fresh, columns * head_size + post * post_columns, post_columns, axis=1
    )
    all_rows = lax.all_gather(line_share, "dp", axis=0, tiled=True)
    wanted = lax.dynamic_slice_in_dim(placing, dp_group * group_reqs, group_reqs)
    held = jnp.arange(dp_size, dtype=jnp.int32)[:, None] * tp_size + line * posts
    held = (held + jnp.arange(posts, dtype=jnp.int32)[None, :]).reshape(1, dp_size * posts)
    mine = choose_rows(jnp.tile(wanted, lines)[:, None] == held, all_rows)
    mine, received = lax.optimization_barrier((mine, received))
    chosen = swap(mine.reshape(lines, group_reqs, share), "y")
    cached = swap(sum_and_copy(chosen, posts), "x").reshape(posts, group_reqs, columns // posts, head_size)
    cached = jnp.transpose(cached, (1, 0, 2, 3)).reshape(group_reqs, columns, head_size)
    query_head_list = cached[:, :heads].reshape(group_reqs, kv_heads, per_group, head_size)
    incoming_key = cached[:, heads : heads + kv_heads][:, :, None, :]
    incoming_value = cached[:, heads + kv_heads :][:, :, None, :]

    slot_ids = tp_lane * slot_dev + jnp.arange(slot_dev, dtype=jnp.int32)
    written = (slot_ids[None, :] == write_pos[:, None])[:, None, :, None]
    key_rows = jnp.where(written, incoming_key, k_cache)
    value_rows = jnp.where(written, incoming_value, value_cache)
    scores = jnp.einsum(
        "rgqd,rgsd->rgqs", query_head_list, key_rows, preferred_element_type=F32
    ) * head_size ** (-0.5)
    is_valid = (slot_ids[None, :] < lengths[:, None])[:, None, None, :]
    masked = jnp.where(is_valid, scores, -1e30)
    local_peak = jnp.max(masked, axis=-1)
    weights = jnp.where(is_valid, jnp.exp(masked - local_peak[..., None]), 0.0)
    local_total = jnp.sum(weights, axis=-1)
    high = lax.reduce_precision(weights, 8, 7)
    halves = jnp.concatenate([high, weights - high], axis=2).astype(BF16)
    local_mixed = jnp.einsum(
        "rgqs,rgsd->rgqd", halves, value_rows, preferred_element_type=F32
    )
    local_mixed = local_mixed[:, :, :per_group] + local_mixed[:, :, per_group:]

    def lane_row(values):
        row = jnp.concatenate(pieces_of(values.reshape(group_reqs, heads)), axis=1)
        return jnp.pad(row, ((0, 0), (0, head_size - row.shape[1])))[:, None, :]

    parts = jnp.concatenate(
        [
            local_mixed.reshape(group_reqs, heads, head_size).astype(BF16),
            lane_row(local_peak),
            lane_row(local_total),
            jnp.zeros((group_reqs, 2, head_size), BF16),
        ],
        axis=1,
    )
    gathered = swap(parts, TP)

    pre_out = expert_units(received.reshape(experts * capacity, width), units)
    gathered, pre_out = lax.optimization_barrier((gathered, pre_out))
    returned = swap(pre_out.reshape(experts, capacity, width), TP)

    tail = gathered[:, heads : heads + 2, : 3 * heads].astype(F32)
    tail = tail[..., :heads] + tail[..., heads : 2 * heads] + tail[..., 2 * heads :]
    peaks, totals = tail[:, 0], tail[:, 1]
    scale = jnp.exp(peaks - jnp.max(peaks, axis=0, keepdims=True))
    total = jnp.sum(scale * totals, axis=0)
    mixed = jnp.sum(scale[:, :, None] * gathered[:, :heads].astype(F32), axis=0)
    attention_row = (mixed / total[:, None]).astype(BF16)

    attention = lax.all_gather(attention_row.reshape(1, width), "x", axis=0, tiled=True)
    projected = contract_rows(attention, out_rows).astype(BF16)
    all_projected = lax.all_gather(projected, "dp", axis=0, tiled=True)
    line_rows = placing.reshape(dp_size, lines, posts)
    line_rows = lax.dynamic_slice_in_dim(line_rows, line, 1, axis=1).reshape(1, dp_size * posts)
    lane_ids = jnp.tile(jnp.arange(group_reqs, dtype=jnp.int32), lines)[:, None]
    from_cache = (dp_group * group_reqs + lane_ids == line_rows).astype(BF16)
    from_line = lane_ids == line * posts + jnp.arange(posts, dtype=jnp.int32)[None, :]
    at_home = jnp.dot(from_cache, all_projected, preferred_element_type=F32)
    at_home = at_home + jnp.dot(from_line.astype(BF16), line_resid, preferred_element_type=F32)
    at_home = at_home.astype(BF16)
    at_home, returned = lax.optimization_barrier((at_home, returned))
    at_home = swap(at_home.reshape(lines, group_reqs, post_columns), "y")
    hidden_all = jnp.transpose(swap(sum_and_copy(at_home, posts), "x"), (1, 0, 2)).reshape(group_reqs, width)
    hidden_f32 = lax.dynamic_slice_in_dim(hidden_all, tp_lane, 1).astype(F32)

    dec_out = expert_units(rms(hidden_all.astype(F32), moe_gain), units)
    dec_back = swap(dec_out.reshape(group_reqs, heads, head_size), TP).astype(F32)
    dec_weight = weight_of[pre_rows:].reshape(experts, 1, 1)
    dec_mixture = jnp.sum(dec_weight * dec_back, axis=0).reshape(1, width)
    out_dec = (hidden_f32 + dec_mixture).astype(BF16)

    flat_back = returned.reshape(experts * capacity, width)
    high, middle, low = pieces_of(weight_of[:pre_rows])

    def mix(piece):
        table = jnp.where(pick, piece[:, :, None], no_value)
        return jnp.dot(
            table.reshape(pre_rows, experts * capacity), flat_back, preferred_element_type=F32
        )

    out_pre = (x_f32 + (mix(high) + mix(middle) + mix(low))).astype(BF16)
    return (out_pre, out_dec)


def solution(mesh):
    groups, lanes = mesh.devices.shape
    lines = min(8, groups)
    fine = Mesh(mesh.devices.reshape(groups, lines, lanes // lines), ("dp", "y", "x"))
    rows = P(("dp", "y", "x"), None)
    units = P(TP, "dp", None)
    cache = P("dp", None, TP, None)
    placed = (rows, rows, rows, P(), P("dp"), P("dp"), cache, cache, P(None, TP))
    placed = placed + (rows, rows, rows, P(), units, units, units)
    return jax.shard_map(
        on_device, mesh=fine, in_specs=placed, out_specs=(rows, rows), check_vma=False
    )
```

```python
import jax
import jax.numpy as jnp
from jax import lax
from jax.sharding import Mesh
from jax.sharding import PartitionSpec as P

TP = ("y", "x")
F32 = jnp.float32
BF16 = jnp.bfloat16


def contract_rows(left_rows, unit_rows):
    return lax.dot_general(
        left_rows, unit_rows, (((1,), (1,)), ((), ())), preferred_element_type=F32
    )


def swap(blocks, axis_name):
    return lax.all_to_all(blocks, axis_name, split_axis=0, concat_axis=0, tiled=True)


def choose_rows(table, rows):
    return jnp.dot(table.astype(BF16), rows, preferred_element_type=F32).astype(BF16)


def pieces_of(x):
    high = lax.reduce_precision(x, 8, 7)
    middle = lax.reduce_precision(x - high, 8, 7)
    low = lax.reduce_precision(x - high - middle, 8, 7)
    return high.astype(BF16), middle.astype(BF16), low.astype(BF16)


def rms(rows_f32, gain):
    mean_square = jnp.mean(rows_f32 * rows_f32, axis=-1, keepdims=True)
    return (rows_f32 * lax.rsqrt(mean_square + 1e-06) * gain).astype(BF16)


def sum_and_copy(parts, copies):
    count, rows, columns = parts.shape
    same = jnp.arange(copies * rows, dtype=jnp.int32)[:, None] % rows
    same = same == jnp.arange(count * rows, dtype=jnp.int32)[None, :] % rows
    return choose_rows(same, parts.reshape(count * rows, columns)).reshape(copies, rows, columns)


def expert_units(rows, units):
    gate = contract_rows(rows, units[0])
    upper = contract_rows(rows, units[1])
    active = (jnp.maximum(gate, 0.0) * upper).astype(BF16)
    return jnp.dot(active, units[2], preferred_element_type=F32).astype(BF16)


def on_device(
    q_new,
    new_key_value,
    resid_dec,
    placing,
    lengths,
    write_pos,
    k_cache,
    value_cache,
    w_out,
    x_pre,
    routes,
    route_scale,
    moe_gain,
    w_gate,
    w_up,
    w_down,
):
    dp_size = lax.axis_size("dp")
    lines, posts = lax.axis_size("y"), lax.axis_size("x")
    tp_size = lines * posts
    dp_group = lax.axis_index("dp")
    line = lax.axis_index("y")
    tp_lane = line * posts + lax.axis_index("x")
    group_reqs, kv_heads, slot_dev, head_size = k_cache.shape
    width = q_new.shape[1]
    heads = width // head_size
    per_group = heads // kv_heads
    total_reqs = placing.shape[0]
    experts = tp_size * w_gate.shape[0]
    assert group_reqs == tp_size and experts == tp_size

    no_value = jnp.zeros((), BF16)
    rows_dev, top_count = routes.shape
    pre_rows = rows_dev - 1
    capacity = min(2 * rows_dev * top_count // experts, rows_dev)
    route_weight = route_scale / jnp.sum(route_scale, axis=-1, keepdims=True)
    expert_ids = jnp.arange(experts, dtype=jnp.int32)
    hits = routes[:, :, None] == expert_ids[None, None, :]
    weight_of = jnp.sum(jnp.where(hits, route_weight[:, :, None], 0.0), axis=1)

    routed = jnp.any(hits[:pre_rows], axis=1)
    row_ids = jnp.arange(pre_rows, dtype=jnp.int32)
    before = (row_ids[None, :] < row_ids[:, None]).astype(BF16)
    position = jnp.dot(before, routed.astype(BF16), preferred_element_type=F32).astype(jnp.int32)
    slots = jnp.arange(capacity, dtype=jnp.int32)
    pick = routed[:, :, None] & (position[:, :, None] == slots[None, None, :])
    pick_table = pick.reshape(pre_rows, experts * capacity)
    x_f32 = x_pre.astype(F32)
    outgoing = lax.dot_general(
        pick_table.astype(BF16),
        lax.optimization_barrier(rms(x_f32, moe_gain)),
        (((0,), (0,)), ((), ())),
        preferred_element_type=F32,
    ).astype(BF16)

    units = lax.all_gather(
        jnp.concatenate([w_gate, w_up, w_down], axis=0), "dp", axis=1, tiled=True
    )

    columns = heads + 2 * kv_heads
    share = columns * head_size // posts
    post = lax.axis_index("x")
    fresh = jnp.concatenate([q_new, new_key_value], axis=1)
    fresh, outgoing = lax.optimization_barrier((fresh, outgoing))
    received = swap(outgoing.reshape(experts, capacity, width), TP)
    line_fresh = lax.all_gather(fresh, "x", axis=0, tiled=True)
    line_share = lax.dynamic_slice_in_dim(line_fresh, post * share, share, axis=1)
    all_rows = lax.all_gather(line_share, "dp", axis=0, tiled=True)
    wanted = lax.dynamic_slice_in_dim(placing, dp_group * group_reqs, group_reqs)
    held = jnp.arange(dp_size, dtype=jnp.int32)[:, None] * tp_size + line * posts
    held = (held + jnp.arange(posts, dtype=jnp.int32)[None, :]).reshape(1, dp_size * posts)
    mine = choose_rows(jnp.tile(wanted, lines)[:, None] == held, all_rows)
    mine, received = lax.optimization_barrier((mine, received))
    chosen = swap(mine.reshape(lines, group_reqs, share), "y")
    cached = swap(sum_and_copy(chosen, posts), "x").reshape(posts, group_reqs, columns // posts, head_size)
    cached = jnp.transpose(cached, (1, 0, 2, 3)).reshape(group_reqs, columns, head_size)
    query_head_list = cached[:, :heads].reshape(group_reqs, kv_heads, per_group, head_size)
    incoming_key = cached[:, heads : heads + kv_heads][:, :, None, :]
    incoming_value = cached[:, heads + kv_heads :][:, :, None, :]

    slot_ids = tp_lane * slot_dev + jnp.arange(slot_dev, dtype=jnp.int32)
    written = (slot_ids[None, :] == write_pos[:, None])[:, None, :, None]
    key_rows = jnp.where(written, incoming_key, k_cache)
    value_rows = jnp.where(written, incoming_value, value_cache)
    scores = jnp.einsum(
        "rgqd,rgsd->rgqs", query_head_list, key_rows, preferred_element_type=F32
    ) * head_size ** (-0.5)
    is_valid = (slot_ids[None, :] < lengths[:, None])[:, None, None, :]
    masked = jnp.where(is_valid, scores, -1e30)
    local_peak = jnp.max(masked, axis=-1)
    weights = jnp.where(is_valid, jnp.exp(masked - local_peak[..., None]), 0.0)
    local_total = jnp.sum(weights, axis=-1)
    high = lax.reduce_precision(weights, 8, 7)
    halves = jnp.concatenate([high, weights - high], axis=2).astype(BF16)
    local_mixed = jnp.einsum(
        "rgqs,rgsd->rgqd", halves, value_rows, preferred_element_type=F32
    )
    local_mixed = local_mixed[:, :, :per_group] + local_mixed[:, :, per_group:]

    def lane_row(values):
        row = jnp.concatenate(pieces_of(values.reshape(group_reqs, heads)), axis=1)
        return jnp.pad(row, ((0, 0), (0, head_size - row.shape[1])))[:, None, :]

    parts = jnp.concatenate(
        [
            local_mixed.reshape(group_reqs, heads, head_size).astype(BF16),
            lane_row(local_peak),
            lane_row(local_total),
            jnp.zeros((group_reqs, 2, head_size), BF16),
        ],
        axis=1,
    )
    gathered = swap(parts, TP)

    tail = gathered[:, heads : heads + 2, : 3 * heads].astype(F32)
    tail = tail[..., :heads] + tail[..., heads : 2 * heads] + tail[..., 2 * heads :]
    peaks, totals = tail[:, 0], tail[:, 1]
    scale = jnp.exp(peaks - jnp.max(peaks, axis=0, keepdims=True))
    total = jnp.sum(scale * totals, axis=0)
    mixed = jnp.sum(scale[:, :, None] * gathered[:, :heads].astype(F32), axis=0)
    attention_row = (mixed / total[:, None]).astype(BF16)

    rows = jnp.concatenate([attention_row, resid_dec.reshape(heads, head_size)], axis=0)
    group_rows = swap(jnp.broadcast_to(rows[None], (tp_size,) + rows.shape), TP)

    pre_out = expert_units(received.reshape(experts * capacity, width), units)
    group_rows, pre_out = lax.optimization_barrier((group_rows, pre_out))
    returned = swap(pre_out.reshape(experts, capacity, width), TP)

    attention = group_rows[:, :heads].reshape(group_reqs, width)
    resid_rows = group_rows[:, heads:].reshape(group_reqs, width)
    projected = jnp.dot(attention, w_out, preferred_element_type=F32).astype(BF16)
    all_projected = lax.all_gather(projected, "dp", axis=0, tiled=True)
    home_ids = dp_group * group_reqs + jnp.arange(group_reqs, dtype=jnp.int32)
    at_home = choose_rows(home_ids[:, None] == placing[None, :], all_projected)
    at_home, returned = lax.optimization_barrier((at_home, returned))
    packed = at_home.reshape(heads, head_size)
    packed = swap(jnp.broadcast_to(packed[None], (tp_size,) + packed.shape), TP)
    proj_home = packed.reshape(tp_size, group_reqs, width // tp_size)
    proj_home = jnp.transpose(proj_home, (1, 0, 2)).reshape(group_reqs, width)
    hidden_all = (resid_rows.astype(F32) + proj_home.astype(F32)).astype(BF16)
    hidden_f32 = lax.dynamic_slice_in_dim(hidden_all, tp_lane, 1).astype(F32)

    dec_out = expert_units(rms(hidden_all.astype(F32), moe_gain), units)
    dec_back = swap(dec_out.reshape(group_reqs, heads, head_size), TP).astype(F32)
    dec_weight = weight_of[pre_rows:].reshape(experts, 1, 1)
    dec_mixture = jnp.sum(dec_weight * dec_back, axis=0).reshape(1, width)
    out_dec = (hidden_f32 + dec_mixture).astype(BF16)

    flat_back = returned.reshape(experts * capacity, width)
    high, middle, low = pieces_of(weight_of[:pre_rows])

    def mix(piece):
        table = jnp.where(pick, piece[:, :, None], no_value)
        return jnp.dot(
            table.reshape(pre_rows, experts * capacity), flat_back, preferred_element_type=F32
        )

    out_pre = (x_f32 + (mix(high) + mix(middle) + mix(low))).astype(BF16)
    return (out_pre, out_dec)


def solution(mesh):
    groups, lanes = mesh.devices.shape
    lines = min(8, groups)
    fine = Mesh(mesh.devices.reshape(groups, lines, lanes // lines), ("dp", "y", "x"))
    rows = P(("dp", "y", "x"), None)
    units = P(TP, "dp", None)
    cache = P("dp", None, TP, None)
    placed = (rows, rows, rows, P(), P("dp"), P("dp"), cache, cache, P(None, TP))
    placed = placed + (rows, rows, rows, P(), units, units, units)
    return jax.shard_map(
        on_device, mesh=fine, in_specs=placed, out_specs=(rows, rows), check_vma=False
    )
```

```python
import jax
import jax.numpy as jnp
from jax import lax
from jax.sharding import Mesh
from jax.sharding import PartitionSpec as P

TP = ("y", "x")
F32 = jnp.float32
BF16 = jnp.bfloat16


def contract_rows(left_rows, unit_rows):
    return lax.dot_general(
        left_rows, unit_rows, (((1,), (1,)), ((), ())), preferred_element_type=F32
    )


def swap(blocks, axis_name):
    return lax.all_to_all(blocks, axis_name, split_axis=0, concat_axis=0, tiled=True)


def choose_rows(table, rows):
    return jnp.dot(table.astype(BF16), rows, preferred_element_type=F32).astype(BF16)


def pieces_of(x):
    high = lax.reduce_precision(x, 8, 7)
    middle = lax.reduce_precision(x - high, 8, 7)
    low = lax.reduce_precision(x - high - middle, 8, 7)
    return high.astype(BF16), middle.astype(BF16), low.astype(BF16)


def rms(rows_f32, gain):
    mean_square = jnp.mean(rows_f32 * rows_f32, axis=-1, keepdims=True)
    return (rows_f32 * lax.rsqrt(mean_square + 1e-06) * gain).astype(BF16)


def sum_and_copy(parts, copies):
    count, rows, columns = parts.shape
    same = jnp.arange(copies * rows, dtype=jnp.int32)[:, None] % rows
    same = same == jnp.arange(count * rows, dtype=jnp.int32)[None, :] % rows
    return choose_rows(same, parts.reshape(count * rows, columns)).reshape(copies, rows, columns)


def expert_units(rows, units):
    gate = contract_rows(rows, units[0])
    upper = contract_rows(rows, units[1])
    active = (jnp.maximum(gate, 0.0) * upper).astype(BF16)
    return jnp.dot(active, units[2], preferred_element_type=F32).astype(BF16)


def on_device(
    q_new,
    new_key_value,
    resid_dec,
    placing,
    lengths,
    write_pos,
    k_cache,
    value_cache,
    w_out,
    x_pre,
    routes,
    route_scale,
    moe_gain,
    w_gate,
    w_up,
    w_down,
):
    dp_size = lax.axis_size("dp")
    lines, posts = lax.axis_size("y"), lax.axis_size("x")
    tp_size = lines * posts
    dp_group = lax.axis_index("dp")
    line = lax.axis_index("y")
    tp_lane = line * posts + lax.axis_index("x")
    group_reqs, kv_heads, slot_dev, head_size = k_cache.shape
    width = q_new.shape[1]
    heads = width // head_size
    per_group = heads // kv_heads
    total_reqs = placing.shape[0]
    experts = tp_size * w_gate.shape[0]
    assert group_reqs == tp_size and experts == tp_size

    no_value = jnp.zeros((), BF16)
    rows_dev, top_count = routes.shape
    pre_rows = rows_dev - 1
    capacity = min(2 * rows_dev * top_count // experts, rows_dev)
    route_weight = route_scale / jnp.sum(route_scale, axis=-1, keepdims=True)
    expert_ids = jnp.arange(experts, dtype=jnp.int32)
    hits = routes[:, :, None] == expert_ids[None, None, :]
    weight_of = jnp.sum(jnp.where(hits, route_weight[:, :, None], 0.0), axis=1)

    routed = jnp.any(hits[:pre_rows], axis=1)
    row_ids = jnp.arange(pre_rows, dtype=jnp.int32)
    before = (row_ids[None, :] < row_ids[:, None]).astype(BF16)
    position = jnp.dot(before, routed.astype(BF16), preferred_element_type=F32).astype(jnp.int32)
    slots = jnp.arange(capacity, dtype=jnp.int32)
    pick = routed[:, :, None] & (position[:, :, None] == slots[None, None, :])
    pick_table = pick.reshape(pre_rows, experts * capacity)
    x_f32 = x_pre.astype(F32)
    outgoing = lax.dot_general(
        pick_table.astype(BF16),
        lax.optimization_barrier(rms(x_f32, moe_gain)),
        (((0,), (0,)), ((), ())),
        preferred_element_type=F32,
    ).astype(BF16)

    units = lax.all_gather(
        jnp.concatenate([w_gate, w_up, w_down], axis=0), "dp", axis=1, tiled=True
    )

    columns = heads + 2 * kv_heads
    share = columns * head_size // posts
    post = lax.axis_index("x")
    fresh = jnp.concatenate([q_new, new_key_value], axis=1)
    fresh, outgoing = lax.optimization_barrier((fresh, outgoing))
    received = swap(outgoing.reshape(experts, capacity, width), TP)
    line_fresh = lax.all_gather(fresh, "x", axis=0, tiled=True)
    line_share = lax.dynamic_slice_in_dim(line_fresh, post * share, share, axis=1)
    all_rows = lax.all_gather(line_share, "dp", axis=0, tiled=True)
    wanted = lax.dynamic_slice_in_dim(placing, dp_group * group_reqs, group_reqs)
    held = jnp.arange(dp_size, dtype=jnp.int32)[:, None] * tp_size + line * posts
    held = (held + jnp.arange(posts, dtype=jnp.int32)[None, :]).reshape(1, dp_size * posts)
    mine = choose_rows(jnp.tile(wanted, lines)[:, None] == held, all_rows)
    mine, received = lax.optimization_barrier((mine, received))
    chosen = swap(mine.reshape(lines, group_reqs, share), "y")
    cached = swap(sum_and_copy(chosen, posts), "x").reshape(posts, group_reqs, columns // posts, head_size)
    cached = jnp.transpose(cached, (1, 0, 2, 3)).reshape(group_reqs, columns, head_size)
    query_head_list = cached[:, :heads].reshape(group_reqs, kv_heads, per_group, head_size)
    incoming_key = cached[:, heads : heads + kv_heads][:, :, None, :]
    incoming_value = cached[:, heads + kv_heads :][:, :, None, :]

    slot_ids = tp_lane * slot_dev + jnp.arange(slot_dev, dtype=jnp.int32)
    written = (slot_ids[None, :] == write_pos[:, None])[:, None, :, None]
    key_rows = jnp.where(written, incoming_key, k_cache)
    value_rows = jnp.where(written, incoming_value, value_cache)
    scores = jnp.einsum(
        "rgqd,rgsd->rgqs", query_head_list, key_rows, preferred_element_type=F32
    ) * head_size ** (-0.5)
    is_valid = (slot_ids[None, :] < lengths[:, None])[:, None, None, :]
    masked = jnp.where(is_valid, scores, -1e30)
    local_peak = jnp.max(masked, axis=-1)
    weights = jnp.where(is_valid, jnp.exp(masked - local_peak[..., None]), 0.0)
    local_total = jnp.sum(weights, axis=-1)
    high = lax.reduce_precision(weights, 8, 7)
    halves = jnp.concatenate([high, weights - high], axis=2).astype(BF16)
    local_mixed = jnp.einsum(
        "rgqs,rgsd->rgqd", halves, value_rows, preferred_element_type=F32
    )
    local_mixed = local_mixed[:, :, :per_group] + local_mixed[:, :, per_group:]

    def lane_row(values):
        row = jnp.concatenate(pieces_of(values.reshape(group_reqs, heads)), axis=1)
        return jnp.pad(row, ((0, 0), (0, head_size - row.shape[1])))[:, None, :]

    parts = jnp.concatenate(
        [
            local_mixed.reshape(group_reqs, heads, head_size).astype(BF16),
            lane_row(local_peak),
            lane_row(local_total),
            jnp.zeros((group_reqs, 2, head_size), BF16),
        ],
        axis=1,
    )
    gathered = swap(parts, TP)

    tail = gathered[:, heads : heads + 2, : 3 * heads].astype(F32)
    tail = tail[..., :heads] + tail[..., heads : 2 * heads] + tail[..., 2 * heads :]
    peaks, totals = tail[:, 0], tail[:, 1]
    scale = jnp.exp(peaks - jnp.max(peaks, axis=0, keepdims=True))
    total = jnp.sum(scale * totals, axis=0)
    mixed = jnp.sum(scale[:, :, None] * gathered[:, :heads].astype(F32), axis=0)
    attention_row = (mixed / total[:, None]).astype(BF16)

    rows = jnp.concatenate([attention_row, resid_dec.reshape(heads, head_size)], axis=0)
    group_rows = swap(jnp.broadcast_to(rows[None], (tp_size,) + rows.shape), TP)

    pre_out = expert_units(received.reshape(experts * capacity, width), units)
    group_rows, pre_out = lax.optimization_barrier((group_rows, pre_out))
    returned = swap(pre_out.reshape(experts, capacity, width), TP)

    attention = group_rows[:, :heads].reshape(group_reqs, width)
    resid_rows = group_rows[:, heads:].reshape(group_reqs, width)
    projected = jnp.dot(attention, w_out, preferred_element_type=F32).astype(BF16)
    all_projected = lax.all_gather(projected, "dp", axis=0, tiled=True)
    home_ids = dp_group * group_reqs + jnp.arange(group_reqs, dtype=jnp.int32)
    at_home = choose_rows(home_ids[:, None] == placing[None, :], all_projected)
    at_home, returned = lax.optimization_barrier((at_home, returned))
    packed = at_home.reshape(heads, head_size)
    packed = swap(jnp.broadcast_to(packed[None], (tp_size,) + packed.shape), TP)
    proj_home = packed.reshape(tp_size, group_reqs, width // tp_size)
    proj_home = jnp.transpose(proj_home, (1, 0, 2)).reshape(group_reqs, width)
    hidden_all = (resid_rows.astype(F32) + proj_home.astype(F32)).astype(BF16)
    own_row = lax.dynamic_slice_in_dim(hidden_all, tp_lane, 1)

    dec_out = expert_units(rms(hidden_all.astype(F32), moe_gain), units)
    own_row, dec_out = lax.optimization_barrier((own_row, dec_out))
    dec_back = swap(dec_out.reshape(group_reqs, heads, head_size), TP).astype(F32)
    dec_weight = weight_of[pre_rows:].reshape(experts, 1, 1)
    dec_mixture = jnp.sum(dec_weight * dec_back, axis=0).reshape(1, width)
    out_dec = (own_row.astype(F32) + dec_mixture).astype(BF16)

    flat_back = returned.reshape(experts * capacity, width)
    high, middle, low = pieces_of(weight_of[:pre_rows])

    def mix(piece):
        table = jnp.where(pick, piece[:, :, None], no_value)
        return jnp.dot(
            table.reshape(pre_rows, experts * capacity), flat_back, preferred_element_type=F32
        )

    out_pre = (x_f32 + (mix(high) + mix(middle) + mix(low))).astype(BF16)
    return (out_pre, out_dec)


def solution(mesh):
    groups, lanes = mesh.devices.shape
    lines = min(8, groups)
    fine = Mesh(mesh.devices.reshape(groups, lines, lanes // lines), ("dp", "y", "x"))
    rows = P(("dp", "y", "x"), None)
    units = P(TP, "dp", None)
    cache = P("dp", None, TP, None)
    placed = (rows, rows, rows, P(), P("dp"), P("dp"), cache, cache, P(None, TP))
    placed = placed + (rows, rows, rows, P(), units, units, units)
    return jax.shard_map(
        on_device, mesh=fine, in_specs=placed, out_specs=(rows, rows), check_vma=False
    )
```

```python
import jax
import jax.numpy as jnp
from jax import lax
from jax.sharding import Mesh
from jax.sharding import PartitionSpec as P

TP = ("y", "x")
F32 = jnp.float32
BF16 = jnp.bfloat16


def contract_rows(left_rows, unit_rows):
    return lax.dot_general(
        left_rows, unit_rows, (((1,), (1,)), ((), ())), preferred_element_type=F32
    )


def swap(blocks, axis_name):
    return lax.all_to_all(blocks, axis_name, split_axis=0, concat_axis=0, tiled=True)


def choose_rows(table, rows):
    return jnp.dot(table.astype(BF16), rows, preferred_element_type=F32).astype(BF16)


def pieces_of(x):
    high = lax.reduce_precision(x, 8, 7)
    middle = lax.reduce_precision(x - high, 8, 7)
    low = lax.reduce_precision(x - high - middle, 8, 7)
    return high.astype(BF16), middle.astype(BF16), low.astype(BF16)


def rms(rows_f32, gain):
    mean_square = jnp.mean(rows_f32 * rows_f32, axis=-1, keepdims=True)
    return (rows_f32 * lax.rsqrt(mean_square + 1e-06) * gain).astype(BF16)


def sum_and_copy(parts, copies):
    count, rows, columns = parts.shape
    same = jnp.arange(copies * rows, dtype=jnp.int32)[:, None] % rows
    same = same == jnp.arange(count * rows, dtype=jnp.int32)[None, :] % rows
    return choose_rows(same, parts.reshape(count * rows, columns)).reshape(copies, rows, columns)


def expert_units(rows, units, gate):
    upper = contract_rows(rows, units[1])
    active = (jnp.maximum(gate, 0.0) * upper).astype(BF16)
    return jnp.dot(active, units[2], preferred_element_type=F32).astype(BF16)


def on_device(
    q_new,
    new_key_value,
    resid_dec,
    placing,
    lengths,
    write_pos,
    k_cache,
    value_cache,
    w_out,
    x_pre,
    routes,
    route_scale,
    moe_gain,
    w_gate,
    w_up,
    w_down,
):
    dp_size = lax.axis_size("dp")
    lines, posts = lax.axis_size("y"), lax.axis_size("x")
    tp_size = lines * posts
    dp_group = lax.axis_index("dp")
    line = lax.axis_index("y")
    tp_lane = line * posts + lax.axis_index("x")
    group_reqs, kv_heads, slot_dev, head_size = k_cache.shape
    width = q_new.shape[1]
    heads = width // head_size
    per_group = heads // kv_heads
    total_reqs = placing.shape[0]
    experts = tp_size * w_gate.shape[0]
    assert group_reqs == tp_size and experts == tp_size

    no_value = jnp.zeros((), BF16)
    rows_dev, top_count = routes.shape
    pre_rows = rows_dev - 1
    capacity = min(2 * rows_dev * top_count // experts, rows_dev)
    route_weight = route_scale / jnp.sum(route_scale, axis=-1, keepdims=True)
    expert_ids = jnp.arange(experts, dtype=jnp.int32)
    hits = routes[:, :, None] == expert_ids[None, None, :]
    weight_of = jnp.sum(jnp.where(hits, route_weight[:, :, None], 0.0), axis=1)

    routed = jnp.any(hits[:pre_rows], axis=1)
    row_ids = jnp.arange(pre_rows, dtype=jnp.int32)
    before = (row_ids[None, :] < row_ids[:, None]).astype(BF16)
    position = jnp.dot(before, routed.astype(BF16), preferred_element_type=F32).astype(jnp.int32)
    slots = jnp.arange(capacity, dtype=jnp.int32)
    pick = routed[:, :, None] & (position[:, :, None] == slots[None, None, :])
    pick_table = pick.reshape(pre_rows, experts * capacity)
    x_f32 = x_pre.astype(F32)
    outgoing = lax.dot_general(
        pick_table.astype(BF16),
        lax.optimization_barrier(rms(x_f32, moe_gain)),
        (((0,), (0,)), ((), ())),
        preferred_element_type=F32,
    ).astype(BF16)

    stored, outgoing = lax.optimization_barrier(((w_gate, w_up, w_down), outgoing))
    units = lax.all_gather(jnp.concatenate(stored, axis=0), "dp", axis=1, tiled=True)

    columns = heads + 2 * kv_heads
    share = columns * head_size // posts
    post = lax.axis_index("x")
    fresh = jnp.concatenate([q_new, new_key_value], axis=1)
    fresh, outgoing = lax.optimization_barrier((fresh, outgoing))
    received = swap(outgoing.reshape(experts, capacity, width), TP)
    line_fresh = lax.all_gather(fresh, "x", axis=0, tiled=True)
    line_share = lax.dynamic_slice_in_dim(line_fresh, post * share, share, axis=1)
    all_rows = lax.all_gather(line_share, "dp", axis=0, tiled=True)
    wanted = lax.dynamic_slice_in_dim(placing, dp_group * group_reqs, group_reqs)
    held = jnp.arange(dp_size, dtype=jnp.int32)[:, None] * tp_size + line * posts
    held = (held + jnp.arange(posts, dtype=jnp.int32)[None, :]).reshape(1, dp_size * posts)
    mine = choose_rows(jnp.tile(wanted, lines)[:, None] == held, all_rows)
    mine, received = lax.optimization_barrier((mine, received))
    chosen = swap(mine.reshape(lines, group_reqs, share), "y")
    cached = swap(sum_and_copy(chosen, posts), "x").reshape(posts, group_reqs, columns // posts, head_size)
    cached = jnp.transpose(cached, (1, 0, 2, 3)).reshape(group_reqs, columns, head_size)
    query_head_list = cached[:, :heads].reshape(group_reqs, kv_heads, per_group, head_size)
    incoming_key = cached[:, heads : heads + kv_heads][:, :, None, :]
    incoming_value = cached[:, heads + kv_heads :][:, :, None, :]

    slot_ids = tp_lane * slot_dev + jnp.arange(slot_dev, dtype=jnp.int32)
    written = (slot_ids[None, :] == write_pos[:, None])[:, None, :, None]
    key_rows = jnp.where(written, incoming_key, k_cache)
    value_rows = jnp.where(written, incoming_value, value_cache)
    scores = jnp.einsum(
        "rgqd,rgsd->rgqs", query_head_list, key_rows, preferred_element_type=F32
    ) * head_size ** (-0.5)
    is_valid = (slot_ids[None, :] < lengths[:, None])[:, None, None, :]
    masked = jnp.where(is_valid, scores, -1e30)
    local_peak = jnp.max(masked, axis=-1)
    weights = jnp.where(is_valid, jnp.exp(masked - local_peak[..., None]), 0.0)
    local_total = jnp.sum(weights, axis=-1)
    high = lax.reduce_precision(weights, 8, 7)
    halves = jnp.concatenate([high, weights - high], axis=2).astype(BF16)
    local_mixed = jnp.einsum(
        "rgqs,rgsd->rgqd", halves, value_rows, preferred_element_type=F32
    )
    local_mixed = local_mixed[:, :, :per_group] + local_mixed[:, :, per_group:]

    def lane_row(values):
        row = jnp.concatenate(pieces_of(values.reshape(group_reqs, heads)), axis=1)
        return jnp.pad(row, ((0, 0), (0, head_size - row.shape[1])))[:, None, :]

    parts = jnp.concatenate(
        [
            local_mixed.reshape(group_reqs, heads, head_size).astype(BF16),
            lane_row(local_peak),
            lane_row(local_total),
            jnp.zeros((group_reqs, 2, head_size), BF16),
        ],
        axis=1,
    )
    gathered = swap(parts, TP)
    arrived = received.reshape(experts * capacity, width)
    gathered, gate = lax.optimization_barrier((gathered, contract_rows(arrived, units[0])))

    tail = gathered[:, heads : heads + 2, : 3 * heads].astype(F32)
    tail = tail[..., :heads] + tail[..., heads : 2 * heads] + tail[..., 2 * heads :]
    peaks, totals = tail[:, 0], tail[:, 1]
    scale = jnp.exp(peaks - jnp.max(peaks, axis=0, keepdims=True))
    total = jnp.sum(scale * totals, axis=0)
    mixed = jnp.sum(scale[:, :, None] * gathered[:, :heads].astype(F32), axis=0)
    attention_row = (mixed / total[:, None]).astype(BF16)

    rows = jnp.concatenate([attention_row, resid_dec.reshape(heads, head_size)], axis=0)
    group_rows = swap(jnp.broadcast_to(rows[None], (tp_size,) + rows.shape), TP)

    pre_out = expert_units(arrived, units, gate)
    group_rows, pre_out = lax.optimization_barrier((group_rows, pre_out))
    returned = swap(pre_out.reshape(experts, capacity, width), TP)

    attention = group_rows[:, :heads].reshape(group_reqs, width)
    resid_rows = group_rows[:, heads:].reshape(group_reqs, width)
    projected = jnp.dot(attention, w_out, preferred_element_type=F32).astype(BF16)
    all_projected = lax.all_gather(projected, "dp", axis=0, tiled=True)
    home_ids = dp_group * group_reqs + jnp.arange(group_reqs, dtype=jnp.int32)
    at_home = choose_rows(home_ids[:, None] == placing[None, :], all_projected)
    at_home, returned = lax.optimization_barrier((at_home, returned))
    packed = at_home.reshape(heads, head_size)
    packed = swap(jnp.broadcast_to(packed[None], (tp_size,) + packed.shape), TP)
    proj_home = packed.reshape(tp_size, group_reqs, width // tp_size)
    proj_home = jnp.transpose(proj_home, (1, 0, 2)).reshape(group_reqs, width)
    hidden_all = (resid_rows.astype(F32) + proj_home.astype(F32)).astype(BF16)
    own_row = lax.dynamic_slice_in_dim(hidden_all, tp_lane, 1)

    normed_dec = rms(hidden_all.astype(F32), moe_gain)
    dec_out = expert_units(normed_dec, units, contract_rows(normed_dec, units[0]))
    own_row, dec_out = lax.optimization_barrier((own_row, dec_out))
    dec_back = swap(dec_out.reshape(group_reqs, heads, head_size), TP).astype(F32)
    dec_weight = weight_of[pre_rows:].reshape(experts, 1, 1)
    dec_mixture = jnp.sum(dec_weight * dec_back, axis=0).reshape(1, width)
    out_dec = (own_row.astype(F32) + dec_mixture).astype(BF16)

    flat_back = returned.reshape(experts * capacity, width)
    high, middle, low = pieces_of(weight_of[:pre_rows])

    def mix(piece):
        table = jnp.where(pick, piece[:, :, None], no_value)
        return jnp.dot(
            table.reshape(pre_rows, experts * capacity), flat_back, preferred_element_type=F32
        )

    out_pre = (x_f32 + (mix(high) + mix(middle) + mix(low))).astype(BF16)
    return (out_pre, out_dec)


def solution(mesh):
    groups, lanes = mesh.devices.shape
    lines = min(8, groups)
    fine = Mesh(mesh.devices.reshape(groups, lines, lanes // lines), ("dp", "y", "x"))
    rows = P(("dp", "y", "x"), None)
    units = P(TP, "dp", None)
    cache = P("dp", None, TP, None)
    placed = (rows, rows, rows, P(), P("dp"), P("dp"), cache, cache, P(None, TP))
    placed = placed + (rows, rows, rows, P(), units, units, units)
    return jax.shard_map(
        on_device, mesh=fine, in_specs=placed, out_specs=(rows, rows), check_vma=False
    )
```

```python
import jax
import jax.numpy as jnp
from jax import lax
from jax.sharding import Mesh
from jax.sharding import PartitionSpec as P

TP = ("y", "x")
F32 = jnp.float32
BF16 = jnp.bfloat16


def contract_rows(left_rows, unit_rows):
    return lax.dot_general(
        left_rows, unit_rows, (((1,), (1,)), ((), ())), preferred_element_type=F32
    )


def swap(blocks, axis_name):
    return lax.all_to_all(blocks, axis_name, split_axis=0, concat_axis=0, tiled=True)


def choose_rows(table, rows):
    return jnp.dot(table.astype(BF16), rows, preferred_element_type=F32).astype(BF16)


def pieces_of(x):
    high = lax.reduce_precision(x, 8, 7)
    middle = lax.reduce_precision(x - high, 8, 7)
    low = lax.reduce_precision(x - high - middle, 8, 7)
    return high.astype(BF16), middle.astype(BF16), low.astype(BF16)


def rms(rows_f32, gain):
    mean_square = jnp.mean(rows_f32 * rows_f32, axis=-1, keepdims=True)
    return (rows_f32 * lax.rsqrt(mean_square + 1e-06) * gain).astype(BF16)


def sum_and_copy(parts, copies):
    count, rows, columns = parts.shape
    same = jnp.arange(copies * rows, dtype=jnp.int32)[:, None] % rows
    same = same == jnp.arange(count * rows, dtype=jnp.int32)[None, :] % rows
    return choose_rows(same, parts.reshape(count * rows, columns)).reshape(copies, rows, columns)


def expert_units(rows, units, gate):
    upper = contract_rows(rows, units[1])
    active = (jnp.maximum(gate, 0.0) * upper).astype(BF16)
    return jnp.dot(active, units[2], preferred_element_type=F32).astype(BF16)


def on_device(
    q_new,
    new_key_value,
    resid_dec,
    placing,
    lengths,
    write_pos,
    k_cache,
    value_cache,
    w_out,
    x_pre,
    routes,
    route_scale,
    moe_gain,
    w_gate,
    w_up,
    w_down,
):
    dp_size = lax.axis_size("dp")
    lines, posts = lax.axis_size("y"), lax.axis_size("x")
    tp_size = lines * posts
    dp_group = lax.axis_index("dp")
    line = lax.axis_index("y")
    tp_lane = line * posts + lax.axis_index("x")
    group_reqs, kv_heads, slot_dev, head_size = k_cache.shape
    width = q_new.shape[1]
    heads = width // head_size
    per_group = heads // kv_heads
    total_reqs = placing.shape[0]
    experts = tp_size * w_gate.shape[0]
    assert group_reqs == tp_size and experts == tp_size

    no_value = jnp.zeros((), BF16)
    rows_dev, top_count = routes.shape
    pre_rows = rows_dev - 1
    capacity = min(2 * rows_dev * top_count // experts, rows_dev)
    route_weight = route_scale / jnp.sum(route_scale, axis=-1, keepdims=True)
    expert_ids = jnp.arange(experts, dtype=jnp.int32)
    hits = routes[:, :, None] == expert_ids[None, None, :]
    weight_of = jnp.sum(jnp.where(hits, route_weight[:, :, None], 0.0), axis=1)

    routed = jnp.any(hits[:pre_rows], axis=1)
    row_ids = jnp.arange(pre_rows, dtype=jnp.int32)
    before = (row_ids[None, :] < row_ids[:, None]).astype(BF16)
    position = jnp.dot(before, routed.astype(BF16), preferred_element_type=F32).astype(jnp.int32)
    slots = jnp.arange(capacity, dtype=jnp.int32)
    pick = routed[:, :, None] & (position[:, :, None] == slots[None, None, :])
    pick_table = pick.reshape(pre_rows, experts * capacity)
    x_f32 = x_pre.astype(F32)
    outgoing = lax.dot_general(
        pick_table.astype(BF16),
        lax.optimization_barrier(rms(x_f32, moe_gain)),
        (((0,), (0,)), ((), ())),
        preferred_element_type=F32,
    ).astype(BF16)

    stored, outgoing = lax.optimization_barrier(((w_gate, w_up, w_down), outgoing))
    units = lax.all_gather(jnp.concatenate(stored, axis=0), "dp", axis=1, tiled=True)

    columns = heads + 2 * kv_heads
    share = columns * head_size // posts
    post = lax.axis_index("x")
    fresh = jnp.concatenate([q_new, new_key_value], axis=1)
    fresh, outgoing = lax.optimization_barrier((fresh, outgoing))
    received = swap(outgoing.reshape(experts, capacity, width), TP)
    line_fresh = lax.all_gather(fresh, "x", axis=0, tiled=True)
    line_share = lax.dynamic_slice_in_dim(line_fresh, post * share, share, axis=1)
    all_rows = lax.all_gather(line_share, "dp", axis=0, tiled=True)
    wanted = lax.dynamic_slice_in_dim(placing, dp_group * group_reqs, group_reqs)
    held = jnp.arange(dp_size, dtype=jnp.int32)[:, None] * tp_size + line * posts
    held = (held + jnp.arange(posts, dtype=jnp.int32)[None, :]).reshape(1, dp_size * posts)
    mine = choose_rows(jnp.tile(wanted, lines)[:, None] == held, all_rows)
    mine, received = lax.optimization_barrier((mine, received))
    chosen = swap(mine.reshape(lines, group_reqs, share), "y")
    cached = swap(sum_and_copy(chosen, posts), "x").reshape(posts, group_reqs, columns // posts, head_size)
    cached = jnp.transpose(cached, (1, 0, 2, 3)).reshape(group_reqs, columns, head_size)
    query_head_list = cached[:, :heads].reshape(group_reqs, kv_heads, per_group, head_size)
    incoming_key = cached[:, heads : heads + kv_heads][:, :, None, :]
    incoming_value = cached[:, heads + kv_heads :][:, :, None, :]

    slot_ids = tp_lane * slot_dev + jnp.arange(slot_dev, dtype=jnp.int32)
    written = (slot_ids[None, :] == write_pos[:, None])[:, None, :, None]
    key_rows = jnp.where(written, incoming_key, k_cache)
    value_rows = jnp.where(written, incoming_value, value_cache)
    scores = jnp.einsum(
        "rgqd,rgsd->rgqs", query_head_list, key_rows, preferred_element_type=F32
    ) * head_size ** (-0.5)
    is_valid = (slot_ids[None, :] < lengths[:, None])[:, None, None, :]
    masked = jnp.where(is_valid, scores, -1e30)
    local_peak = jnp.max(masked, axis=-1)
    weights = jnp.where(is_valid, jnp.exp(masked - local_peak[..., None]), 0.0)
    local_total = jnp.sum(weights, axis=-1)
    high = lax.reduce_precision(weights, 8, 7)
    halves = jnp.concatenate([high, weights - high], axis=2).astype(BF16)
    local_mixed = jnp.einsum(
        "rgqs,rgsd->rgqd", halves, value_rows, preferred_element_type=F32
    )
    local_mixed = local_mixed[:, :, :per_group] + local_mixed[:, :, per_group:]

    def lane_row(values):
        row = jnp.concatenate(pieces_of(values.reshape(group_reqs, heads)), axis=1)
        return jnp.pad(row, ((0, 0), (0, head_size - row.shape[1])))[:, None, :]

    parts = jnp.concatenate(
        [
            local_mixed.reshape(group_reqs, heads, head_size).astype(BF16),
            lane_row(local_peak),
            lane_row(local_total),
            jnp.zeros((group_reqs, 2, head_size), BF16),
        ],
        axis=1,
    )
    gathered = swap(parts, TP)
    arrived = received.reshape(experts * capacity, width)
    gathered, gate = lax.optimization_barrier((gathered, contract_rows(arrived, units[0])))

    tail = gathered[:, heads : heads + 2, : 3 * heads].astype(F32)
    tail = tail[..., :heads] + tail[..., heads : 2 * heads] + tail[..., 2 * heads :]
    peaks, totals = tail[:, 0], tail[:, 1]
    scale = jnp.exp(peaks - jnp.max(peaks, axis=0, keepdims=True))
    total = jnp.sum(scale * totals, axis=0)
    mixed = jnp.sum(scale[:, :, None] * gathered[:, :heads].astype(F32), axis=0)
    attention_row = (mixed / total[:, None]).astype(BF16)

    rows = jnp.concatenate([attention_row, resid_dec.reshape(heads, head_size)], axis=0)
    group_rows = swap(jnp.broadcast_to(rows[None], (tp_size,) + rows.shape), TP)

    pre_out = expert_units(arrived, units, gate)
    group_rows, pre_out = lax.optimization_barrier((group_rows, pre_out))
    returned = swap(pre_out.reshape(experts, capacity, width), TP)

    attention = group_rows[:, :heads].reshape(group_reqs, width)
    resid_rows = group_rows[:, heads:].reshape(group_reqs, width)
    projected = jnp.dot(attention, w_out, preferred_element_type=F32).astype(BF16)
    all_projected = lax.all_gather(projected, "dp", axis=0, tiled=True)
    home_ids = dp_group * group_reqs + jnp.arange(group_reqs, dtype=jnp.int32)
    at_home = choose_rows(home_ids[:, None] == placing[None, :], all_projected)
    at_home, returned = lax.optimization_barrier((at_home, returned))
    packed = at_home.reshape(heads, head_size)
    packed = swap(jnp.broadcast_to(packed[None], (tp_size,) + packed.shape), TP)
    proj_home = packed.reshape(tp_size, group_reqs, width // tp_size)
    proj_home = jnp.transpose(proj_home, (1, 0, 2)).reshape(group_reqs, width)
    proj_home = lax.optimization_barrier(proj_home)
    hidden_all = (resid_rows.astype(F32) + proj_home.astype(F32)).astype(BF16)
    own_row = lax.dynamic_slice_in_dim(hidden_all, tp_lane, 1)

    normed_dec = rms(hidden_all.astype(F32), moe_gain)
    dec_out = expert_units(normed_dec, units, contract_rows(normed_dec, units[0]))
    own_row, dec_out = lax.optimization_barrier((own_row, dec_out))
    dec_back = swap(dec_out.reshape(group_reqs, heads, head_size), TP).astype(F32)
    dec_weight = weight_of[pre_rows:].reshape(experts, 1, 1)
    dec_mixture = jnp.sum(dec_weight * dec_back, axis=0).reshape(1, width)
    out_dec = (own_row.astype(F32) + dec_mixture).astype(BF16)

    flat_back = returned.reshape(experts * capacity, width)
    high, middle, low = pieces_of(weight_of[:pre_rows])

    def mix(piece):
        table = jnp.where(pick, piece[:, :, None], no_value)
        return jnp.dot(
            table.reshape(pre_rows, experts * capacity), flat_back, preferred_element_type=F32
        )

    out_pre = (x_f32 + (mix(high) + mix(middle) + mix(low))).astype(BF16)
    return (out_pre, out_dec)


def solution(mesh):
    groups, lanes = mesh.devices.shape
    lines = min(8, groups)
    fine = Mesh(mesh.devices.reshape(groups, lines, lanes // lines), ("dp", "y", "x"))
    rows = P(("dp", "y", "x"), None)
    units = P(TP, "dp", None)
    cache = P("dp", None, TP, None)
    placed = (rows, rows, rows, P(), P("dp"), P("dp"), cache, cache, P(None, TP))
    placed = placed + (rows, rows, rows, P(), units, units, units)
    return jax.shard_map(
        on_device, mesh=fine, in_specs=placed, out_specs=(rows, rows), check_vma=False
    )
```
